32 devices in a mesh: dp: 16 (over z, y, core), tensor: 2 (over x).
Axes of the slice: x: 2, y: 2, z: 4, core: 2. Of those that a mesh axis runs over, the one named last changes fastest.
Arguments:
- patches: bfloat16 [50176, 768], P(('dp', 'tensor')), may hold values from -6 to 6
- visible: int32 [1024, 49], P(('dp', 'tensor')), may hold values from 0 to 195, as said below
- pos_table: float32 [196, 768], replicated, may hold values from -6 to 6
- cotangent: bfloat16 [50176, 768], P(('dp', 'tensor')), may hold values from -6 to 6
- step_count: int32 [1], replicated, may hold values from 2 to 20
- w_qkv: float32 [768, 3, 768], P('dp', None, 'tensor'), may hold values from -0.21875 to 0.21875
- m_qkv: float32 [768, 3, 768], P('dp', None, 'tensor'), may hold values from -0.00018793954 to 0.00018793954
- v_qkv: float32 [768, 3, 768], P('dp', None, 'tensor'), may hold values from 7.48811e-09 to 2.9669868e-08
- w_proj: float32 [768, 768], P('tensor', 'dp'), may hold values from -0.875 to 0.875
- m_proj: float32 [768, 768], P('tensor', 'dp'), may hold values from -0.00018793954 to 0.00018793954
- v_proj: float32 [768, 768], P('tensor', 'dp'), may hold values from 7.48811e-09 to 2.9669868e-08
- w_fc1: float32 [768, 4, 768], P('dp', None, 'tensor'), may hold values from -0.21875 to 0.21875
- m_fc1: float32 [768, 4, 768], P('dp', None, 'tensor'), may hold values from -0.00018793954 to 0.00018793954
- v_fc1: float32 [768, 4, 768], P('dp', None, 'tensor'), may hold values from 7.48811e-09 to 2.9669868e-08
- w_fc2: float32 [4, 768, 768], P(None, 'tensor', 'dp'), may hold values from -0.109375 to 0.109375
- m_fc2: float32 [4, 768, 768], P(None, 'tensor', 'dp'), may hold values from -0.00018793954 to 0.00018793954
- v_fc2: float32 [4, 768, 768], P(None, 'tensor', 'dp'), may hold values from 7.48811e-09 to 2.9669868e-08
- split_bias: float32 [6, 768], P(None, 'tensor'), may hold values from -3 to 3
- m_split: float32 [6, 768], P(None, 'tensor'), may hold values from -0.0005638186 to 0.0005638186
- v_split: float32 [6, 768], P(None, 'tensor'), may hold values from 6.640399e-08 to 2.6844165e-07
- norm_bias: float32 [6, 768], replicated, may hold values from -1.2 to 1.8
- m_norm: float32 [6, 768], replicated, may hold values from -0.0005638186 to 0.0005638186
- v_norm: float32 [6, 768], replicated, may hold values from 6.640399e-08 to 2.6844165e-07
Outputs:
- block_out: bfloat16 [50176, 768], P(('dp', 'tensor'))
- input_grad: float32 [50176, 768], P(('dp', 'tensor'))
- grad_norm: float32 [], replicated
- new_qkv: float32 [768, 3, 768], P('dp', None, 'tensor')
- first_qkv: float32 [768, 3, 768], P('dp', None, 'tensor')
- second_qkv: float32 [768, 3, 768], P('dp', None, 'tensor')
- new_proj: float32 [768, 768], P('tensor', 'dp')
- first_proj: float32 [768, 768], P('tensor', 'dp')
- second_proj: float32 [768, 768], P('tensor', 'dp')
- new_fc1: float32 [768, 4, 768], P('dp', None, 'tensor')
- first_fc1: float32 [768, 4, 768], P('dp', None, 'tensor')
- second_fc1: float32 [768, 4, 768], P('dp', None, 'tensor')
- new_fc2: float32 [4, 768, 768], P(None, 'tensor', 'dp')
- first_fc2: float32 [4, 768, 768], P(None, 'tensor', 'dp')
- second_fc2: float32 [4, 768, 768], P(None, 'tensor', 'dp')
- new_split: float32 [6, 768], P(None, 'tensor')
- first_split: float32 [6, 768], P(None, 'tensor')
- second_split: float32 [6, 768], P(None, 'tensor')
- new_norm: float32 [6, 768], replicated
- first_norm: float32 [6, 768], replicated
- second_norm: float32 [6, 768], replicated
The draws below stay inside these ranges and needn't reach their ends.
Inputs may be any that keep to these rules, and one draw needn't show every extreme that they name: `visible`: the 49 entries of an image are distinct patch positions.
All inputs are finite; a program needn't handle non-finite values.
Results may differ from the reference program's by a relative error of at most 0.014.
Values may be sent and summed in bfloat16 or wider, within the bound.
No kernel may reach another device: no remote copies, remote signals or barrier semaphores. Data moves between devices by JAX's collectives and lax.ppermute only.
A program may use at most 256 MiB of HBM per device.

```python
import math
import jax
import jax.numpy as jnp
from jax import lax

D = 768
HEADS = 12
HD = 64
FF = 3072
PATCHES = 196
VISIBLE = 49
IMG_DEV = 64
IMAGES = 1024
TOKENS = 50176


def draw_visible(key, part):
    image_keys = jax.random.split(key, IMAGES)

    def pick_patches(image_key):
        return jax.random.permutation(image_key, PATCHES)[:VISIBLE]
    return jax.vmap(pick_patches)(image_keys).astype(jnp.int32)


def draw_norm_bias(key, part):
    noise = jnp.clip(jax.random.normal(key, (6, D), jnp.float32), -4.0, 4.0)
    row_index = jnp.arange(6)[:, None]
    gain_rows = (row_index == 0) | (row_index == 3)
    return jnp.where(gain_rows, 1.0 + 0.2 * noise, 0.3 * noise).astype(jnp.float32)


def steps_of(own_key, dims, cuts, smallest, high):
    def one(axis_at, shards_of):
        draws = jax.random.uniform(jax.random.fold_in(jax.random.fold_in(own_key, 6), axis_at), (shards_of,), jnp.float32, smallest / len(cuts), high / len(cuts))
        return jnp.repeat(jnp.exp(draws), dims[axis_at] // shards_of).reshape((-1,) + (1,) * (len(dims) - axis_at - 1))

    gain = one(*cuts[0])
    for cut in cuts[1:]:
        gain = gain * one(*cut)
    return gain


def gaussian(rng, extent, spread, most, cuts=(), kind=jnp.bfloat16):
    array = spread * jax.random.normal(rng, extent, jnp.float32)
    if cuts:
        array = array * steps_of(rng, extent, cuts, -0.22, 0.18)
    return jnp.clip(array, -most, most).astype(kind)


def setup_inputs(seed: int = 0) -> dict:
    key_of = jax.random.split(jax.random.key(seed), 24)
    return {
        "patches": gaussian(key_of[0], (TOKENS, D), 1.0, 6.0, ((0, 32),)),
        "visible": draw_visible(jax.random.fold_in(key_of[23], 71), 0),
        "pos_table": gaussian(key_of[2], (PATCHES, D), 1.0, 6.0, (), jnp.float32),
        "cotangent": gaussian(key_of[3], (TOKENS, D), 1.0, 6.0, ((0, 32),)),
        "step_count": jax.random.randint(key_of[4], (1,), 2, 21).astype(jnp.int32),
        "w_qkv": gaussian(key_of[5], (D, 3, D), D ** -0.5, 0.21875, ((0, 16), (2, 2)), jnp.float32),
        "m_qkv": gaussian(key_of[6], (D, 3, D), (0.11 / (12 * D * D) ** 0.5), 0.00018793954, ((0, 16), (2, 2)), jnp.float32),
        "v_qkv": jnp.clip(jnp.exp(math.log(2.9669868339965433e-08) - 1.3768156 * jax.random.uniform(key_of[7], (D, 3, D), jnp.float32) ** steps_of(key_of[7], (D, 3, D), ((0, 16), (2, 2)), -0.2, 0.2)), 7.488109687869837e-09, 2.9669868339965433e-08),
        "w_proj": gaussian(key_of[8], (D, D), (D // 16) ** -0.5, 0.875, ((0, 2), (1, 16)), jnp.float32),
        "m_proj": gaussian(key_of[9], (D, D), (0.11 / (12 * D * D) ** 0.5), 0.00018793954, ((0, 2), (1, 16)), jnp.float32),
        "v_proj": jnp.clip(jnp.exp(math.log(2.9669868339965433e-08) - 1.3768156 * jax.random.uniform(key_of[10], (D, D), jnp.float32) ** steps_of(key_of[10], (D, D), ((0, 2), (1, 16)), -0.2, 0.2)), 7.488109687869837e-09, 2.9669868339965433e-08),
        "w_fc1": gaussian(key_of[11], (D, 4, D), D ** -0.5, 0.21875, ((0, 16), (2, 2)), jnp.float32),
        "m_fc1": gaussian(key_of[12], (D, 4, D), (0.11 / (12 * D * D) ** 0.5), 0.00018793954, ((0, 16), (2, 2)), jnp.float32),
        "v_fc1": jnp.clip(jnp.exp(math.log(2.9669868339965433e-08) - 1.3768156 * jax.random.uniform(key_of[13], (D, 4, D), jnp.float32) ** steps_of(key_of[13], (D, 4, D), ((0, 16), (2, 2)), -0.2, 0.2)), 7.488109687869837e-09, 2.9669868339965433e-08),
        "w_fc2": gaussian(key_of[14], (4, D, D), FF ** -0.5, 0.109375, ((1, 2), (2, 16)), jnp.float32),
        "m_fc2": gaussian(key_of[15], (4, D, D), (0.11 / (12 * D * D) ** 0.5), 0.00018793954, ((1, 2), (2, 16)), jnp.float32),
        "v_fc2": jnp.clip(jnp.exp(math.log(2.9669868339965433e-08) - 1.3768156 * jax.random.uniform(key_of[16], (4, D, D), jnp.float32) ** steps_of(key_of[16], (4, D, D), ((1, 2), (2, 16)), -0.2, 0.2)), 7.488109687869837e-09, 2.9669868339965433e-08),
        "split_bias": gaussian(key_of[17], (6, D), 0.5, 3.0, ((1, 2),), jnp.float32),
        "m_split": gaussian(key_of[18], (6, D), (0.33 / (12 * D * D) ** 0.5), 0.0005638186, ((1, 2),), jnp.float32),
        "v_split": jnp.clip(jnp.exp(math.log(2.6844165290640376e-07) - 1.3968764 * jax.random.uniform(key_of[19], (6, D), jnp.float32) ** steps_of(key_of[19], (6, D), ((1, 2),), -0.2, 0.2)), 6.640399163870825e-08, 2.6844165290640376e-07),
        "norm_bias": draw_norm_bias(jax.random.fold_in(key_of[23], 71), 0),
        "m_norm": gaussian(key_of[21], (6, D), (0.33 / (12 * D * D) ** 0.5), 0.0005638186, (), jnp.float32),
        "v_norm": jnp.clip(jnp.exp(jax.random.uniform(key_of[22], (6, D), jnp.float32, math.log(6.640399163870825e-08), math.log(2.6844165290640376e-07))), 6.640399163870825e-08, 2.6844165290640376e-07),
    }


@jax.custom_vjp
def low(v):
    return lax.optimization_barrier(v.astype(jnp.bfloat16)).astype(jnp.float32)

@jax.custom_vjp
def low_back(v):
    return v

def low_keep(v):
    return (low(v), None)

def low_pass(kept, grad):
    return (grad,)

def back_keep(v):
    return (v, None)

def back_low(kept, grad):
    return (low(grad),)
low.defvjp(low_keep, low_pass)
low_back.defvjp(back_keep, back_low)
norm_eps = 1e-06
beta_one = 0.9
beta_two = 0.95
adam_eps = 1e-08
clip_value = 1.0
matrix_rate = 0.02
proj_rate = 0.08
vector_rate = 0.2
matrix_decay = 0.05
highest = lax.Precision.HIGHEST

def layer_norm(values, row_gain, row_shift):
    row_mean = lax.optimization_barrier(jnp.mean(values, axis=-1, keepdims=True))
    centred = values - row_mean
    variance = lax.optimization_barrier(jnp.mean(centred * centred, axis=-1, keepdims=True))
    return centred * lax.rsqrt(variance + norm_eps) * row_gain + row_shift

def forward(inputs, w_qkv, w_proj, w_fc1, w_fc2, split_bias, norm_bias):
    rows_total = inputs.shape[0]
    image_count = rows_total // VISIBLE
    head_shape = (image_count, VISIBLE, HEADS, HD)
    attn_scale = HD ** (-0.5)
    qkv_flat = low(w_qkv).reshape(D, 3 * D)
    proj_low = low(w_proj)
    fc1_flat = low(w_fc1).reshape(D, FF)
    fc2_flat = low(w_fc2).reshape(FF, D)
    normed = low(layer_norm(inputs, norm_bias[0], norm_bias[1]))
    projected = jnp.dot(normed, qkv_flat, precision=highest)
    queries = low(low_back(projected[:, :D] + split_bias[0]))
    keys_low = low(low_back(projected[:, D:2 * D]))
    values_low = low(low_back(projected[:, 2 * D:] + split_bias[1]))
    query_heads = queries.reshape(head_shape)
    key_heads = keys_low.reshape(head_shape)
    value_heads = values_low.reshape(head_shape)
    scores = low_back(jnp.einsum('bqhd,bkhd->bhqk', query_heads, key_heads, precision=highest) * attn_scale)
    soft_low = low(jax.nn.softmax(scores, axis=-1))
    mixed_low = low(low_back(jnp.einsum('bhqk,bkhd->bqhd', soft_low, value_heads, precision=highest).reshape(rows_total, D)))
    attended = low_back(jnp.dot(mixed_low, proj_low, precision=highest) + norm_bias[2])
    hidden_res = inputs + attended
    normed_two = low(layer_norm(hidden_res, norm_bias[3], norm_bias[4]))
    pre_gelu = low_back(jnp.dot(normed_two, fc1_flat, precision=highest) + split_bias[2:].reshape(FF))
    activated = low(jax.nn.gelu(pre_gelu, approximate=False))
    ffn_out = low_back(jnp.dot(activated, fc2_flat, precision=highest) + norm_bias[5])
    return hidden_res + ffn_out

def adam_update(weight, gradient, first_moment, second, factor, bias_first, bias_second, learn_rate, decay_rate):
    clipped = gradient * factor
    first_new = beta_one * first_moment + (1.0 - beta_one) * clipped
    second_new = beta_two * second + (1.0 - beta_two) * clipped * clipped
    direction = first_new / bias_first / (jnp.sqrt(second_new / bias_second) + adam_eps)
    return (weight - learn_rate * (direction + decay_rate * weight), first_new, second_new)

def reference(patches, visible, pos_table, cotangent, step_count, w_qkv, m_qkv, v_qkv, w_proj, m_proj, v_proj, w_fc1, m_fc1, v_fc1, w_fc2, m_fc2, v_fc2, split_bias, m_split, v_split, norm_bias, m_norm, v_norm):
    inputs = patches.astype(jnp.float32) + jnp.take(pos_table, visible.reshape(-1).astype(jnp.int32), axis=0)
    group_rows = IMG_DEV * VISIBLE
    groups = inputs.shape[0] // group_rows
    group_inputs = inputs.reshape(groups, group_rows, D)
    group_cot = cotangent.astype(jnp.float32).reshape(groups, group_rows, D)
    params = (w_qkv, w_proj, w_fc1, w_fc2, split_bias, norm_bias)

    def group_step(totals, paired):
        block_in, block_cot = paired
        result, pullback = jax.vjp(forward, block_in, *params)
        grads = pullback(block_cot)
        summed = tuple((total_part + grad_part for total_part, grad_part in zip(totals, grads[1:])))
        return (summed, (result.astype(jnp.bfloat16), grads[0]))
    zeros = tuple((jnp.zeros_like(param) for param in params))
    totals, (outputs, input_grads) = lax.scan(group_step, zeros, (group_inputs, group_cot))
    squares = jnp.sum(totals[0] * totals[0])
    for gradient in totals[1:]:
        squares = squares + jnp.sum(gradient * gradient)
    grad_norm = jnp.sqrt(squares)
    factor = jnp.minimum(1.0, clip_value / (grad_norm + 1e-06))
    step_value = step_count[0].astype(jnp.float32)
    bias_first = 1.0 - jnp.power(beta_one, step_value)
    bias_second = 1.0 - jnp.power(beta_two, step_value)
    qkv_out = adam_update(w_qkv, totals[0], m_qkv, v_qkv, factor, bias_first, bias_second, matrix_rate, matrix_decay)
    proj_out = adam_update(w_proj, totals[1], m_proj, v_proj, factor, bias_first, bias_second, proj_rate, matrix_decay)
    fc1_out = adam_update(w_fc1, totals[2], m_fc1, v_fc1, factor, bias_first, bias_second, matrix_rate, matrix_decay)
    fc2_out = adam_update(w_fc2, totals[3], m_fc2, v_fc2, factor, bias_first, bias_second, matrix_rate, matrix_decay)
    split_out = adam_update(split_bias, totals[4], m_split, v_split, factor, bias_first, bias_second, vector_rate, 0.0)
    norm_out = adam_update(norm_bias, totals[5], m_norm, v_norm, factor, bias_first, bias_second, vector_rate, 0.0)
    return (outputs.reshape(-1, D), input_grads.reshape(-1, D), grad_norm, qkv_out[0], qkv_out[1], qkv_out[2], proj_out[0], proj_out[1], proj_out[2], fc1_out[0], fc1_out[1], fc1_out[2], fc2_out[0], fc2_out[1], fc2_out[2], split_out[0], split_out[1], split_out[2], norm_out[0], norm_out[1], norm_out[2])
```

```python
import jax
import jax.numpy as jnp
from jax import lax
from jax.sharding import PartitionSpec as P

HD = 64
VISIBLE = 49


norm_eps = 1e-06
beta_one = 0.9
beta_two = 0.95
adam_eps = 1e-08
clip_value = 1.0
matrix_rate = 0.02
proj_rate = 0.08
vector_rate = 0.2
matrix_decay = 0.05


def layer_norm(values, row_gain, row_shift):
    row_mean = jnp.mean(values, axis=-1, keepdims=True)
    centred = values - row_mean
    variance = jnp.mean(centred * centred, axis=-1, keepdims=True)
    return centred * lax.rsqrt(variance + norm_eps) * row_gain + row_shift


def adam_update(
    weight, gradient, first_moment, second, factor, bias_first, bias_second, learn_rate, decay_rate
):
    clipped = gradient * factor
    first_new = beta_one * first_moment + (1.0 - beta_one) * clipped
    second_new = beta_two * second + (1.0 - beta_two) * clipped * clipped
    direction = first_new / bias_first / (jnp.sqrt(second_new / bias_second) + adam_eps)
    return (weight - learn_rate * (direction + decay_rate * weight), first_new, second_new)


def transpose_dot(left_side, right_side):
    return lax.dot_general(
        left_side, right_side, (((0,), (0,)), ((), ())), preferred_element_type=jnp.float32
    )


def dot_back(left_side, right_side):
    return lax.dot_general(
        left_side, right_side, (((1,), (1,)), ((), ())), preferred_element_type=jnp.float32
    )


def square_sum(arrays):
    total = jnp.sum(arrays[0] * arrays[0])
    for member in arrays[1:]:
        total = total + jnp.sum(member * member)
    return total


def standard_normal(values):
    cumulative = 0.5 + 0.5 * lax.erf(values * (0.5**0.5))
    density = jnp.exp(-0.5 * values * values) * (0.5 / jnp.pi) ** 0.5
    return cumulative, density


def body(
    patches,
    visible,
    pos_table,
    cotangent,
    step_count,
    w_qkv,
    m_qkv,
    v_qkv,
    w_proj,
    m_proj,
    v_proj,
    w_fc1,
    m_fc1,
    v_fc1,
    w_fc2,
    m_fc2,
    v_fc2,
    split_bias,
    m_split,
    v_split,
    norm_bias,
    m_norm,
    v_norm,
):
    model_width = patches.shape[1]
    shard_rows = w_qkv.shape[0]
    shard_width = w_qkv.shape[2]
    halves = model_width // shard_width
    attn_scale = HD ** (-0.5)
    full_rows = patches.shape[0]
    every = ("tensor", "dp")
    low_type = jnp.bfloat16

    def rows_of(proj_like):
        return jnp.swapaxes(proj_like, -1, -2)

    def gather(block):
        whole = lax.all_gather(block.astype(low_type), every, axis=0, tiled=True)
        return whole.reshape(halves, model_width, block.shape[1])

    fc2_rows = jnp.transpose(w_fc2, (2, 0, 1)).reshape(shard_rows, 4 * shard_width)
    qkv_low = gather(w_qkv.reshape(shard_rows, 3 * shard_width))
    rest_low = gather(
        jnp.concatenate(
            [rows_of(w_proj), w_fc1.reshape(shard_rows, 4 * shard_width), fc2_rows], axis=1
        )
    )
    proj_low = [rest_low[t, :, :shard_width] for t in range(halves)]
    fc1_low = [rest_low[t, :, shard_width : 5 * shard_width] for t in range(halves)]
    fc2_low = [rest_low[t, :, 5 * shard_width :] for t in range(halves)]
    split_whole_bias = lax.all_gather(split_bias, "tensor", axis=0, tiled=False)

    inputs = patches.astype(jnp.float32) + jnp.take(pos_table, visible.reshape(-1), axis=0)
    normed, norm_back = jax.vjp(layer_norm, inputs, norm_bias[0], norm_bias[1])
    normed_low = normed.astype(low_type)
    heads_here = shard_width // HD
    head_shape = (full_rows // VISIBLE, VISIBLE, heads_here, HD)
    attended = jnp.zeros((full_rows, model_width), jnp.float32)
    kept = []
    for t in range(halves):
        projected = jnp.dot(normed_low, qkv_low[t], preferred_element_type=jnp.float32)
        bias_t = split_whole_bias[t]
        query_heads = (projected[:, :shard_width] + bias_t[0]).astype(low_type).reshape(head_shape)
        key_heads = projected[:, shard_width : 2 * shard_width].astype(low_type).reshape(head_shape)
        value_heads = (
            (projected[:, 2 * shard_width :] + bias_t[1]).astype(low_type).reshape(head_shape)
        )
        scores = (
            jnp.einsum(
                "bqhd,bkhd->bhqk", query_heads, key_heads, preferred_element_type=jnp.float32
            )
            * attn_scale
        )
        attention = jax.nn.softmax(scores, axis=-1)
        soft_low = attention.astype(low_type)
        mixed_low = (
            jnp.einsum(
                "bhqk,bkhd->bqhd", soft_low, value_heads, preferred_element_type=jnp.float32
            )
            .reshape(full_rows, shard_width)
            .astype(low_type)
        )
        attended = attended + dot_back(mixed_low, proj_low[t])
        kept.append((query_heads, key_heads, value_heads, attention, soft_low, mixed_low))
    hidden_res = inputs + (attended + norm_bias[2])
    normed_two, norm_two_back = jax.vjp(layer_norm, hidden_res, norm_bias[3], norm_bias[4])
    normed_two_low = normed_two.astype(low_type)
    ffn_out = jnp.zeros((full_rows, model_width), jnp.float32)
    grad_out = cotangent.astype(jnp.float32)
    grad_normed_two = jnp.zeros((full_rows, model_width), jnp.float32)
    grad_fc1, grad_fc2, grad_fc1_bias = [], [], []
    for t in range(halves):
        pre_gelu = jnp.dot(
            normed_two_low, fc1_low[t], preferred_element_type=jnp.float32
        ) + split_whole_bias[t, 2:].reshape(-1)
        cumulative, density = standard_normal(pre_gelu)
        activated_low = (pre_gelu * cumulative).astype(low_type)
        slope_low = (cumulative + pre_gelu * density).astype(low_type)
        ffn_out = ffn_out + dot_back(activated_low, fc2_low[t])
        grad_fc2.append(transpose_dot(cotangent, activated_low).astype(low_type))
        grad_act = jnp.dot(cotangent, fc2_low[t], preferred_element_type=jnp.float32)
        grad_pre = (grad_act * slope_low.astype(jnp.float32)).astype(low_type)
        grad_fc1.append(transpose_dot(normed_two_low, grad_pre).astype(low_type))
        grad_fc1_bias.append(jnp.sum(grad_pre.astype(jnp.float32), axis=0).reshape(4, shard_width))
        grad_normed_two = grad_normed_two + dot_back(grad_pre, fc1_low[t])
    block_out = (hidden_res + (ffn_out + norm_bias[5])).astype(low_type)

    def scatter(parts):
        stacked = jnp.stack(parts).reshape(halves * model_width, parts[0].shape[1])
        return lax.psum_scatter(stacked, every, scatter_dimension=0, tiled=True).astype(jnp.float32)

    ffn_shard = scatter(
        [jnp.concatenate([grad_fc1[t], grad_fc2[t]], axis=1) for t in range(halves)]
    )
    grad_hidden_norm, grad_gain_two, grad_shift_two = norm_two_back(grad_normed_two)
    grad_hidden = grad_out + grad_hidden_norm
    grad_attn_low = grad_hidden.astype(low_type)
    grad_normed = jnp.zeros((full_rows, model_width), jnp.float32)
    grad_front, grad_query_bias = [], []
    for t in range(halves):
        query_heads, key_heads, value_heads, attention, soft_low, mixed_low = kept[t]
        grad_proj = transpose_dot(grad_attn_low, mixed_low).astype(low_type)
        grad_mixed = (
            jnp.dot(grad_attn_low, proj_low[t], preferred_element_type=jnp.float32)
            .astype(low_type)
            .reshape(head_shape)
        )
        grad_soft = jnp.einsum(
            "bqhd,bkhd->bhqk", grad_mixed, value_heads, preferred_element_type=jnp.float32
        )
        grad_values = jnp.einsum(
            "bhqk,bqhd->bkhd", soft_low, grad_mixed, preferred_element_type=jnp.float32
        ).astype(low_type)
        grad_scores = (
            attention * (grad_soft - jnp.sum(grad_soft * attention, axis=-1, keepdims=True))
        ).astype(low_type)
        grad_queries = (
            jnp.einsum(
                "bhqk,bkhd->bqhd", grad_scores, key_heads, preferred_element_type=jnp.float32
            )
            * attn_scale
        ).astype(low_type)
        grad_keys = (
            jnp.einsum(
                "bhqk,bqhd->bkhd", grad_scores, query_heads, preferred_element_type=jnp.float32
            )
            * attn_scale
        ).astype(low_type)
        grad_query_rows = grad_queries.reshape(full_rows, shard_width)
        grad_value_rows = grad_values.reshape(full_rows, shard_width)
        grad_proj_in = jnp.concatenate(
            [grad_query_rows, grad_keys.reshape(full_rows, shard_width), grad_value_rows], axis=1
        )
        grad_qkv = transpose_dot(normed_low, grad_proj_in).astype(low_type)
        grad_front.append(jnp.concatenate([grad_qkv, grad_proj], axis=1))
        grad_normed = grad_normed + dot_back(grad_proj_in, qkv_low[t])
        grad_query_bias.append(
            jnp.stack(
                [
                    jnp.sum(grad_query_rows.astype(jnp.float32), axis=0),
                    jnp.sum(grad_value_rows.astype(jnp.float32), axis=0),
                ]
            )
        )
    front_shard = scatter(grad_front)
    grad_input_norm, grad_gain_one, grad_shift_one = norm_back(grad_normed)
    input_grad = grad_hidden + grad_input_norm
    grad_split = jnp.stack(
        [jnp.concatenate([grad_query_bias[t], grad_fc1_bias[t]]) for t in range(halves)]
    )
    grad_norm_rows = jnp.stack(
        [
            grad_gain_one,
            grad_shift_one,
            jnp.sum(grad_attn_low.astype(jnp.float32), axis=0),
            grad_gain_two,
            grad_shift_two,
            jnp.sum(grad_out, axis=0),
        ]
    )
    shards = (
        front_shard[:, : 3 * shard_width].reshape(shard_rows, 3, shard_width),
        rows_of(front_shard[:, 3 * shard_width :]),
        ffn_shard[:, : 4 * shard_width].reshape(shard_rows, 4, shard_width),
        jnp.transpose(
            ffn_shard[:, 4 * shard_width :].reshape(shard_rows, 4, shard_width), (1, 2, 0)
        ),
    )
    local_square = square_sum((front_shard, ffn_shard))
    norm_total, split_whole, square_total = lax.psum(
        (grad_norm_rows, grad_split, local_square), ("dp", "tensor")
    )
    split_total = split_whole[lax.axis_index("tensor")]
    grad_norm = jnp.sqrt(
        square_total + jnp.sum(norm_total * norm_total) + jnp.sum(split_whole * split_whole)
    )
    factor = jnp.minimum(1.0, clip_value / (grad_norm + 1e-06))
    step_value = step_count[0].astype(jnp.float32)
    bias_first = 1.0 - jnp.power(beta_one, step_value)
    bias_second = 1.0 - jnp.power(beta_two, step_value)
    qkv_out = adam_update(
        w_qkv, shards[0], m_qkv, v_qkv, factor, bias_first, bias_second, matrix_rate, matrix_decay
    )
    proj_out = adam_update(
        w_proj, shards[1], m_proj, v_proj, factor, bias_first, bias_second, proj_rate, matrix_decay
    )
    fc1_out = adam_update(
        w_fc1, shards[2], m_fc1, v_fc1, factor, bias_first, bias_second, matrix_rate, matrix_decay
    )
    fc2_out = adam_update(
        w_fc2, shards[3], m_fc2, v_fc2, factor, bias_first, bias_second, matrix_rate, matrix_decay
    )
    split_out = adam_update(
        split_bias, split_total, m_split, v_split, factor, bias_first, bias_second, vector_rate, 0.0
    )
    norm_out = adam_update(
        norm_bias, norm_total, m_norm, v_norm, factor, bias_first, bias_second, vector_rate, 0.0
    )
    return (
        block_out,
        input_grad,
        grad_norm,
        qkv_out[0],
        qkv_out[1],
        qkv_out[2],
        proj_out[0],
        proj_out[1],
        proj_out[2],
        fc1_out[0],
        fc1_out[1],
        fc1_out[2],
        fc2_out[0],
        fc2_out[1],
        fc2_out[2],
        split_out[0],
        split_out[1],
        split_out[2],
        norm_out[0],
        norm_out[1],
        norm_out[2],
    )


def solution(mesh):
    return jax.shard_map(
        body,
        mesh=mesh,
        in_specs=(
            P(("dp", "tensor"), None),
            P(("dp", "tensor"), None),
            P(),
            P(("dp", "tensor"), None),
            P(),
            P("dp", None, "tensor"),
            P("dp", None, "tensor"),
            P("dp", None, "tensor"),
            P("tensor", "dp"),
            P("tensor", "dp"),
            P("tensor", "dp"),
            P("dp", None, "tensor"),
            P("dp", None, "tensor"),
            P("dp", None, "tensor"),
            P(None, "tensor", "dp"),
            P(None, "tensor", "dp"),
            P(None, "tensor", "dp"),
            P(None, "tensor"),
            P(None, "tensor"),
            P(None, "tensor"),
            P(),
            P(),
            P(),
        ),
        out_specs=(
            P(("dp", "tensor"), None),
            P(("dp", "tensor"), None),
            P(),
            P("dp", None, "tensor"),
            P("dp", None, "tensor"),
            P("dp", None, "tensor"),
            P("tensor", "dp"),
            P("tensor", "dp"),
            P("tensor", "dp"),
            P("dp", None, "tensor"),
            P("dp", None, "tensor"),
            P("dp", None, "tensor"),
            P(None, "tensor", "dp"),
            P(None, "tensor", "dp"),
            P(None, "tensor", "dp"),
            P(None, "tensor"),
            P(None, "tensor"),
            P(None, "tensor"),
            P(),
            P(),
            P(),
        ),
        check_vma=False,
    )
```

```python
from functools import partial

import jax
import jax.numpy as jnp
import numpy as np
from jax import lax
from jax.experimental import pallas as pl
from jax.experimental.pallas import tpu as pltpu
from jax.sharding import PartitionSpec as P

HD = 64
VISIBLE = 49


norm_eps = 1e-06
beta_one = 0.9
beta_two = 0.95
adam_eps = 1e-08
clip_value = 1.0
matrix_rate = 0.02
proj_rate = 0.08
vector_rate = 0.2
matrix_decay = 0.05


def layer_norm(values, row_gain, row_shift):
    row_mean = jnp.mean(values, axis=-1, keepdims=True)
    centred = values - row_mean
    variance = jnp.mean(centred * centred, axis=-1, keepdims=True)
    return centred * lax.rsqrt(variance + norm_eps) * row_gain + row_shift


def adam_update(
    weight, gradient, first_moment, second, factor, bias_first, bias_second, learn_rate, decay_rate
):
    clipped = gradient * factor
    first_new = beta_one * first_moment + (1.0 - beta_one) * clipped
    second_new = beta_two * second + (1.0 - beta_two) * clipped * clipped
    direction = first_new / bias_first / (jnp.sqrt(second_new / bias_second) + adam_eps)
    return (weight - learn_rate * (direction + decay_rate * weight), first_new, second_new)


def transpose_dot(left_side, right_side):
    return lax.dot_general(
        left_side, right_side, (((0,), (0,)), ((), ())), preferred_element_type=jnp.float32
    )


def dot_back(left_side, right_side):
    return lax.dot_general(
        left_side, right_side, (((1,), (1,)), ((), ())), preferred_element_type=jnp.float32
    )


def square_sum(arrays):
    total = jnp.sum(arrays[0] * arrays[0])
    for member in arrays[1:]:
        total = total + jnp.sum(member * member)
    return total


def standard_normal(values):
    cumulative = 0.5 + 0.5 * lax.erf(values * (0.5**0.5))
    density = jnp.exp(-0.5 * values * values) * (0.5 / jnp.pi) ** 0.5
    return cumulative, density


every_axis = ("dp", "tensor")
low_type = jnp.bfloat16
wide_type = jnp.float32
WINDOW_IMAGES = 2
QUERY_ROWS = 112
KEY_ROWS = 128
PAIR = 2 * HD
GROUP_IMAGES = 16
GROUP_ROWS = GROUP_IMAGES * VISIBLE
WINDOWS = GROUP_IMAGES // WINDOW_IMAGES
WINDOW_UNROLL = 4
HIDDEN = -1e30


def wide(values):
    return values.astype(wide_type)


class Exchange:
    def __init__(self, dp_size, tensor_size):
        self.total = dp_size * tensor_size
        self.outer = self.total // 8
        flat_dp = lax.axis_index("dp")
        self.across = lax.axis_index("tensor")
        self.core = flat_dp & 1
        self.up = (flat_dp >> 1) & 1
        self.deep = flat_dp >> 2

    def swap(self, value, mask):
        return lax.ppermute(value, every_axis, [(i, i ^ mask) for i in range(self.total)])

    def swap_by_core(self, value, even_mask, odd_mask):
        masks = (even_mask, odd_mask)
        return lax.ppermute(
            value, every_axis, [(i, i ^ masks[(i >> 1) & 1]) for i in range(self.total)]
        )

    def digits(self):
        size = 1
        while size < self.outer:
            radix = 4 if self.outer // size >= 4 else 2
            yield size, radix
            size *= radix

    def spot(self, core, flip_second, flip_first):
        first = jnp.where(core == 0, self.up, self.across) ^ flip_first
        second = jnp.where(core == 0, self.across, self.up) ^ flip_second
        return jnp.where(core == 0, second, first), jnp.where(core == 0, first, second)


def tie(value, *others):
    return lax.optimization_barrier((value,) + tuple(jax.tree.leaves(others)))[0]


def tie_all(values, *others):
    leaves = tuple(jax.tree.leaves(others))
    return list(lax.optimization_barrier(tuple(values) + leaves)[: len(values)])


def deposit(pieces, slots):
    count = len(pieces)
    shape = (count,) + pieces[0].shape

    def kernel(spots, *refs):
        out, done = refs[count], refs[count + 1]
        copies = [
            pltpu.make_async_copy(refs[k], out.at[spots[k]], done.at[k]) for k in range(count)
        ]
        for copy in copies:
            copy.start()
        for copy in copies:
            copy.wait()

    return pl.pallas_call(
        kernel,
        out_shape=jax.ShapeDtypeStruct(shape, pieces[0].dtype),
        grid_spec=pltpu.PrefetchScalarGridSpec(
            num_scalar_prefetch=1,
            grid=(1,),
            in_specs=[pl.BlockSpec(memory_space=pl.ANY)] * count,
            out_specs=pl.BlockSpec(
                shape, lambda i, spots: (0,) * len(shape), pipeline_mode=pl.Buffered(1)
            ),
            scratch_shapes=[pltpu.SemaphoreType.DMA((count,))],
        ),
        name="deposit",
    )(jnp.stack(slots).astype(jnp.int32), *pieces)


def deposit_whole(pieces, slots, widths):
    count = len(pieces)
    outer, rows, _ = pieces[0].shape
    outs = [(t, w) for t in range(2) for w in range(len(widths))]
    starts = [sum(widths[:w]) for w in range(len(widths))]

    def kernel(spots, *refs):
        out, done = refs[count : count + len(outs)], refs[-1]
        copies = []
        for k in range(count):
            for o, (t, w) in enumerate(outs):
                source = refs[k].at[:, :, pl.ds(starts[w], widths[w])]
                target = out[o].at[:, spots[3 * k + 1], spots[3 * k + 2]]
                copy = pltpu.make_async_copy(source, target, done.at[k, w])
                copies.append((spots[3 * k] == t, copy))
        for here, copy in copies:
            pl.when(here)(copy.start)
        for here, copy in copies:
            pl.when(here)(copy.wait)

    shapes = [(outer, 2, 2, rows, widths[w]) for t, w in outs]
    flat = jnp.stack([jnp.asarray(v, jnp.int32) for slot in slots for v in slot])
    whole = pl.pallas_call(
        kernel,
        out_shape=[jax.ShapeDtypeStruct(shape, low_type) for shape in shapes],
        grid_spec=pltpu.PrefetchScalarGridSpec(
            num_scalar_prefetch=1,
            grid=(1,),
            in_specs=[pl.BlockSpec(memory_space=pl.ANY)] * count,
            out_specs=[
                pl.BlockSpec(shape, lambda i, spots: (0,) * 5, pipeline_mode=pl.Buffered(1))
                for shape in shapes
            ],
            scratch_shapes=[pltpu.SemaphoreType.DMA((count, len(widths)))],
        ),
        name="deposit_whole",
    )(flat, *pieces)
    flat_rows = [part.reshape(outer * 4 * rows, part.shape[-1]) for part in whole]
    return [flat_rows[t * len(widths) : (t + 1) * len(widths)] for t in range(2)]


class Gather:
    def __init__(self, ring, block, widths):
        self.ring, self.cur, self.widths = ring, block[None], widths

    def send_deep(self):
        ring = self.ring
        steps = list(ring.digits())
        for size, radix in steps:
            self.spot = (ring.deep // size) % radix
            self.arrived = [ring.swap(self.cur, (k * size) << 3) for k in range(1, radix)]
            if (size, radix) != steps[-1]:
                self.collect()

    def collect(self):
        radix = 1 + len(self.arrived)
        stacked = deposit([self.cur] + self.arrived, [self.spot ^ k for k in range(radix)])
        self.cur = stacked.reshape((radix * self.cur.shape[0],) + self.cur.shape[1:])

    def send_beside(self):
        self.collect()
        self.beside = self.ring.swap_by_core(self.cur, 4, 1)

    def send_far(self):
        self.far = [self.ring.swap_by_core(piece, 1, 4) for piece in (self.cur, self.beside)]

    def send_core(self):
        self.mine = [self.cur, self.beside] + self.far
        self.theirs = [self.ring.swap(piece, 2) for piece in self.mine]

    def whole(self):
        ring = self.ring
        slots = []
        for core in (ring.core, 1 - ring.core):
            for flip_second in range(2):
                for flip_first in range(2):
                    slots.append(ring.spot(core, flip_second, flip_first) + (core,))
        return deposit_whole(self.mine + self.theirs, slots, self.widths)


class Scatter:
    def __init__(self, ring, halves):
        self.ring = ring
        self.rows = halves[0][0].shape[0] // (ring.outer * 4)
        shape = (ring.outer, 2, 2, self.rows)
        self.views = [[p.reshape(shape + p.shape[1:]) for p in parts] for parts in halves]

    def cut(self, t, core, up=None):
        cuts = []
        for view in self.views[t]:
            ups = 2 if up is None else 1
            part = lax.dynamic_slice(
                view,
                (0, 0 if up is None else up, core, 0, 0),
                (view.shape[0], ups, 1) + view.shape[3:],
            )
            cuts.append(part.reshape(view.shape[:1] + (ups,) + view.shape[3:]))
        return cuts[0] if len(cuts) == 1 else jnp.concatenate(cuts, axis=-1)

    def send_core(self):
        self.sent = [self.cut(t, 1 - self.ring.core) for t in range(2)]
        self.arrived = [self.ring.swap(part, 2) for part in self.sent]

    def partial(self, flip_second, flip_first):
        across, up = self.ring.spot(self.ring.core, flip_second, flip_first)
        terms = [
            wide(self.cut(t, self.ring.core, up)[:, 0])
            + wide(lax.dynamic_index_in_dim(self.arrived[t], up, 1, keepdims=False))
            for t in range(2)
        ]
        return jnp.where(across == 0, terms[0], terms[1])

    def send_far(self):
        swap = self.ring.swap_by_core
        self.far = [swap(self.partial(1, k).astype(low_type), 1, 4) for k in (1, 0)]

    def send_near(self):
        near = self.partial(0, 1) + wide(self.far[0])
        self.near = self.ring.swap_by_core(near.astype(low_type), 4, 1)

    def send_deep(self):
        ring = self.ring
        cur = self.partial(0, 0) + wide(self.far[1]) + wide(self.near)
        for size, radix in reversed(list(ring.digits())):
            spot = (ring.deep // size) % radix
            cur = cur.reshape((radix, size) + cur.shape[1:])
            sent = cur.astype(low_type)
            self.deep = [
                ring.swap(
                    lax.dynamic_index_in_dim(sent, spot ^ k, 0, keepdims=False), (k * size) << 3
                )
                for k in range(1, radix)
            ]
            cur = lax.dynamic_index_in_dim(cur, spot, 0, keepdims=False)
            for part in self.deep:
                cur = cur + wide(part)
        self.result = cur.reshape(cur.shape[1:])


def sum_everywhere(ring, value):
    bit = 1
    while bit < ring.total:
        radix = 4 if ring.total // bit >= 4 else 2
        terms = [value] + [ring.swap(value, k * bit) for k in range(1, radix)]
        while len(terms) > 1:
            terms = [terms[i] + terms[i + 1] for i in range(0, len(terms), 2)]
        value = terms[0]
        bit *= radix
    return value


def window_rows(index):
    query_start = (index * (WINDOW_IMAGES * VISIBLE)) // 16 * 16
    key_start = jnp.minimum(query_start, GROUP_ROWS - KEY_ROWS)
    return (
        pl.ds(pl.multiple_of(query_start, 16), QUERY_ROWS),
        pl.ds(pl.multiple_of(key_start, 16), KEY_ROWS),
    )


def window_masks():
    base = np.arange(WINDOWS)[:, None, None] * (WINDOW_IMAGES * VISIBLE)
    query_start = base // 16 * 16
    key_start = np.minimum(query_start, GROUP_ROWS - KEY_ROWS)
    query_at = query_start - base + np.arange(QUERY_ROWS)[None, :, None]
    key_at = key_start - base + np.arange(KEY_ROWS)[None, None, :]
    used = (query_at >= 0) & (query_at < WINDOW_IMAGES * VISIBLE)
    low_key = np.where(query_at < VISIBLE, 0, VISIBLE)
    allowed = used & (key_at >= low_key) & (key_at < low_key + VISIBLE)
    return np.where(allowed, 0.0, HIDDEN).astype(np.float32)


def split_pair(values):
    lane = lax.broadcasted_iota(jnp.int32, values.shape, 1)
    zero = jnp.zeros_like(values)
    return jnp.concatenate(
        [jnp.where(lane < HD, values, zero), jnp.where(lane >= HD, values, zero)], axis=0
    )


def join_pair(stacked):
    lane = lax.broadcasted_iota(jnp.int32, (KEY_ROWS, PAIR), 1)
    return jnp.where(lane < HD, stacked[:KEY_ROWS], stacked[KEY_ROWS:])


def over_windows(window, store):
    def several(step, carry):
        places = [step * WINDOW_UNROLL + offset for offset in range(WINDOW_UNROLL)]
        results = [window(place) for place in places]
        for place, result in zip(places, results):
            store(place, *result)
        return carry

    lax.fori_loop(0, WINDOWS // WINDOW_UNROLL, several, 0)


def head_blocks(shape, head_axis, value):
    own_axis = 1 - head_axis
    lanes = lax.broadcasted_iota(jnp.int32, shape, head_axis) < HD
    stack = lax.broadcasted_iota(jnp.int32, shape, own_axis) < KEY_ROWS
    return jnp.where(lanes == stack, value, 0.0).astype(low_type)


def attention_forward_kernel(queries, keys, values, hide, *refs):
    mixed, soft, scale = refs[-3:]
    mixed[...] = jnp.zeros_like(mixed)
    ones = head_blocks((2 * KEY_ROWS, PAIR), 1, 1.0)

    def window(index):
        query_rows, key_rows = window_rows(index)
        scaled = queries[query_rows, :] * jnp.asarray(HD**-0.5, low_type)
        scores = dot_back(scaled, split_pair(keys[key_rows, :]))
        weights = []
        for head in range(2):
            part = scores[:, head * KEY_ROWS : (head + 1) * KEY_ROWS] + hide[index]
            highest = jnp.maximum(jnp.max(part, axis=-1, keepdims=True), HIDDEN / 4)
            weights.append(jnp.exp(part - highest).astype(low_type))
        weights = jnp.concatenate(weights, axis=1)
        right = jnp.concatenate([split_pair(values[key_rows, :]), ones], axis=1)
        result = jnp.dot(weights, right, preferred_element_type=wide_type)
        total = result[:, PAIR:]
        inverse = jnp.where(total > 0.0, 1.0 / total, 0.0)
        return weights, inverse, (result[:, :PAIR] * inverse).astype(low_type)

    def store(index, weights, inverse, result):
        soft[index, 0] = weights
        scale[index, 0] = inverse
        mixed[window_rows(index)[0], :] += result

    over_windows(window, store)


def attention_backward_kernel(
    queries, keys, values, soft, scale, mixed, grad_mixed, grad_qkv, sums, *, width
):
    group, pair = pl.program_id(0), pl.program_id(1)
    query_cols, key_cols, value_cols = [
        pl.ds(pl.multiple_of(part * width + pair * PAIR, PAIR), PAIR) for part in range(3)
    ]
    minus_ones = head_blocks((2 * KEY_ROWS, PAIR), 1, -1.0)
    for cols in (query_cols, key_cols, value_cols):
        grad_qkv[:, cols] = jnp.zeros((GROUP_ROWS, PAIR), low_type)

        @pl.when(group == 0)
        def _():
            sums[:, cols] = jnp.zeros((8, PAIR), wide_type)

    def window(index):
        query_rows, key_rows = window_rows(index)
        split_keys = split_pair(keys[key_rows, :])
        weights = soft[index, 0]
        grads = wide(grad_mixed[query_rows, :]) * scale[index, 0]
        shares = (grads * wide(mixed[query_rows, :])).astype(low_type)
        grads = grads.astype(low_type)
        left = jnp.concatenate([grads, shares], axis=1)
        right = jnp.concatenate([split_pair(values[key_rows, :]), minus_ones], axis=1)
        grad_scores = (wide(weights) * dot_back(left, right)).astype(low_type)
        grad_queries = (
            jnp.dot(grad_scores, split_keys, preferred_element_type=wide_type) * HD**-0.5
        )
        grad_keys = join_pair(transpose_dot(grad_scores, queries[query_rows, :])) * HD**-0.5
        grad_values = join_pair(transpose_dot(weights, grads))
        return (
            grad_queries.astype(low_type),
            grad_keys.astype(low_type),
            grad_values.astype(low_type),
            jnp.sum(grad_queries.reshape(-1, 8, PAIR), axis=0),
            jnp.sum(grad_values.reshape(-1, 8, PAIR), axis=0),
        )

    def store(index, grad_queries, grad_keys, grad_values, query_sums, value_sums):
        query_rows, key_rows = window_rows(index)
        grad_qkv[query_rows, query_cols] += grad_queries
        grad_qkv[key_rows, key_cols] += grad_keys
        grad_qkv[key_rows, value_cols] += grad_values
        sums[:, query_cols] += query_sums
        sums[:, value_cols] += value_sums

    over_windows(window, store)


def attention_forward(qkv, group, before=()):
    rows, width = qkv.shape[0], qkv.shape[1] // 3
    pairs = width // PAIR
    part = [
        pl.BlockSpec((GROUP_ROWS, PAIR), lambda p, k=k: (group, k * pairs + p)) for k in range(3)
    ]
    hide = window_masks()
    return pl.pallas_call(
        attention_forward_kernel,
        grid=(pairs,),
        in_specs=part
        + [
            pl.BlockSpec(hide.shape, lambda p: (0, 0, 0), pipeline_mode=pl.Buffered(1)),
        ]
        + [pl.BlockSpec(memory_space=pl.ANY)] * len(before),
        out_specs=[
            pl.BlockSpec((GROUP_ROWS, PAIR), lambda p: (group, p)),
            pl.BlockSpec((WINDOWS, 1, QUERY_ROWS, 2 * KEY_ROWS), lambda p: (group, p, 0, 0)),
            pl.BlockSpec((WINDOWS, 1, QUERY_ROWS, PAIR), lambda p: (group, p, 0, 0)),
        ],
        out_shape=[
            jax.ShapeDtypeStruct((rows, width), low_type),
            jax.ShapeDtypeStruct(
                (rows // GROUP_ROWS * WINDOWS, pairs, QUERY_ROWS, 2 * KEY_ROWS), low_type
            ),
            jax.ShapeDtypeStruct((rows // GROUP_ROWS * WINDOWS, pairs, QUERY_ROWS, PAIR), wide_type),
        ],
        input_output_aliases={4 + k: k for k in range(len(before))},
        name="attention_forward",
    )(qkv, qkv, qkv, hide, *before)


def attention_backward(qkv, mixed, soft, scale, grad_mixed):
    rows, width = qkv.shape[0], qkv.shape[1] // 3
    pairs = width // PAIR
    part = [
        pl.BlockSpec((GROUP_ROWS, PAIR), lambda g, p, k=k: (g, k * pairs + p)) for k in range(3)
    ]
    return pl.pallas_call(
        partial(attention_backward_kernel, width=width),
        grid=(rows // GROUP_ROWS, pairs),
        in_specs=part
        + [
            pl.BlockSpec((WINDOWS, 1, QUERY_ROWS, 2 * KEY_ROWS), lambda g, p: (g, p, 0, 0)),
            pl.BlockSpec((WINDOWS, 1, QUERY_ROWS, PAIR), lambda g, p: (g, p, 0, 0)),
            pl.BlockSpec((GROUP_ROWS, PAIR), lambda g, p: (g, p)),
            pl.BlockSpec((GROUP_ROWS, PAIR), lambda g, p: (g, p)),
        ],
        out_specs=[
            pl.BlockSpec((GROUP_ROWS, 3 * width), lambda g, p: (g, 0)),
            pl.BlockSpec((8, 3 * width), lambda g, p: (0, 0)),
        ],
        out_shape=[
            jax.ShapeDtypeStruct((rows, 3 * width), low_type),
            jax.ShapeDtypeStruct((8, 3 * width), wide_type),
        ],
        name="attention_backward",
    )(qkv, qkv, qkv, soft, scale, mixed, grad_mixed)


def body(
    sizes,
    patches,
    visible,
    pos_table,
    cotangent,
    step_count,
    w_qkv,
    m_qkv,
    v_qkv,
    w_proj,
    m_proj,
    v_proj,
    w_fc1,
    m_fc1,
    v_fc1,
    w_fc2,
    m_fc2,
    v_fc2,
    split_bias,
    m_split,
    v_split,
    norm_bias,
    m_norm,
    v_norm,
):
    model_width = patches.shape[1]
    full_rows = patches.shape[0]
    shard_rows = w_qkv.shape[0]
    shard_width = w_qkv.shape[2]
    ring = Exchange(*sizes)
    halves = 2

    def rows_of(proj_like):
        return jnp.swapaxes(proj_like, -1, -2)

    def low(block):
        return block.astype(low_type)

    mid_block = jnp.concatenate(
        [rows_of(w_proj), w_fc1.reshape(shard_rows, 4 * shard_width)], axis=1
    )
    fc2_block = jnp.transpose(w_fc2, (2, 0, 1)).reshape(shard_rows, 4 * shard_width)
    qkv_all = Gather(ring, low(w_qkv.reshape(shard_rows, 3 * shard_width)), [3 * shard_width])
    qkv_all.send_deep()
    qkv_all.send_beside()
    mid_all = Gather(ring, tie(low(mid_block), qkv_all.cur), [shard_width, 4 * shard_width])
    mid_all.send_deep()
    qkv_all.send_far()
    qkv_all.send_core()
    fc2_all = Gather(ring, tie(low(fc2_block), qkv_all.far), [4 * shard_width])
    fc2_all.send_deep()
    qkv_low = [part[0] for part in qkv_all.whole()]
    mid_all.arrived = tie_all(mid_all.arrived, qkv_low)
    mid_all.send_beside()
    other_bias = ring.swap(tie(split_bias, qkv_all.cur), 1)
    split_whole_bias = [
        jnp.where(ring.across == t, split_bias, other_bias) for t in range(halves)
    ]

    inputs = wide(patches) + jnp.take(pos_table, visible.reshape(-1), axis=0)
    inputs = tie(inputs, qkv_all.cur)
    normed, norm_back = jax.vjp(layer_norm, inputs, norm_bias[0], norm_bias[1])
    normed_low = low(normed)
    projections = []
    for t in range(halves):
        bias_t = split_whole_bias[t]
        shift = jnp.concatenate([bias_t[0], jnp.zeros_like(bias_t[0]), bias_t[1]])
        left = tie(normed_low, mid_all.cur)
        projections.append(
            low(jnp.dot(left, qkv_low[t], preferred_element_type=wide_type) + shift)
        )
    mid_all.beside = tie(mid_all.beside, projections)
    mid_all.send_far()
    outcomes = [(), ()]
    groups = full_rows // GROUP_ROWS
    for call in range(halves * groups):
        t, group = call // groups, call % groups
        source = projections[t]
        if call:
            source = tie(source, outcomes[(call - 1) // groups])
        outcomes[t] = attention_forward(source, group, outcomes[t])
        done = outcomes[t]
        if call == 0:
            fc2_all.arrived = tie_all(fc2_all.arrived, done)
            fc2_all.send_beside()
        if call == 1:
            mid_all.far = tie_all(mid_all.far, done)
            mid_all.send_core()
            fc2_all.beside = tie(fc2_all.beside, done)
            fc2_all.send_far()
    mid_all.theirs = tie_all(mid_all.theirs, outcomes)
    proj_low, fc1_low = zip(*mid_all.whole())
    kept = [(projections[t],) + tuple(outcomes[t]) for t in range(halves)]
    attended = norm_bias[2]
    for t in range(halves):
        attended = attended + dot_back(kept[t][1], proj_low[t])
    hidden_res = inputs + attended
    normed_two, norm_two_back = jax.vjp(layer_norm, hidden_res, norm_bias[3], norm_bias[4])
    normed_two_low = low(normed_two)
    fc2_all.far = tie_all(fc2_all.far, normed_two_low)
    fc2_all.send_core()
    grad_out = wide(cotangent)
    activated, slopes, grad_fc2 = [], [], []
    for t in range(halves):
        pre_gelu = jnp.dot(
            normed_two_low, fc1_low[t], preferred_element_type=wide_type
        ) + split_whole_bias[t][2:].reshape(-1)
        cumulative, density = standard_normal(pre_gelu)
        activated.append(low(pre_gelu * cumulative))
        slopes.append(low(cumulative + pre_gelu * density))
        grad_fc2.append(low(transpose_dot(cotangent, activated[t])))
    fc2_all.theirs = tie_all(fc2_all.theirs, activated)
    fc2_low = [part[0] for part in fc2_all.whole()]
    fc2_sum = Scatter(ring, [[g] for g in grad_fc2])
    fc2_sum.send_core()
    cotangent_later = tie(cotangent, fc2_sum.sent)
    grad_pres, grad_fc1, grad_fc1_bias = [], [], []
    for t in range(halves):
        grad_act = jnp.dot(cotangent_later, fc2_low[t], preferred_element_type=wide_type)
        grad_pres.append(low(grad_act * wide(slopes[t])))
        grad_fc1_bias.append(jnp.sum(wide(grad_pres[t]), axis=0).reshape(4, shard_width))
    fc2_sum.arrived = tie_all(fc2_sum.arrived, grad_pres)
    fc2_sum.send_far()
    for t in range(halves):
        grad_fc1.append(low(transpose_dot(normed_two_low, tie(grad_pres[t], fc2_sum.arrived))))
    fc1_sum = Scatter(ring, [[g] for g in grad_fc1])
    fc1_sum.send_core()
    fc2_sum.far = tie_all(fc2_sum.far, grad_fc1)
    fc2_sum.send_near()
    grad_normed_two = 0.0
    for t in range(halves):
        grad_pre = tie(grad_pres[t], fc1_sum.sent, fc2_sum.far)
        grad_normed_two = grad_normed_two + dot_back(grad_pre, fc1_low[t])
    fc2_sum.near = tie(fc2_sum.near, grad_normed_two)
    fc2_sum.send_deep()
    fc1_sum.arrived = tie_all(fc1_sum.arrived, grad_normed_two)
    fc1_sum.send_far()
    grad_hidden_norm, grad_gain_two, grad_shift_two = norm_two_back(
        tie(grad_normed_two, fc1_sum.arrived, fc2_sum.near)
    )
    grad_hidden = grad_out + grad_hidden_norm
    grad_attn_low = low(grad_hidden)
    grad_proj, grad_mixed = [], []
    for t in range(halves):
        grad_proj.append(low(transpose_dot(grad_attn_low, kept[t][1])))
        grad_mixed.append(low(jnp.dot(grad_attn_low, proj_low[t], preferred_element_type=wide_type)))
    grad_proj_ins, grad_front, grad_query_bias = [], [], []
    for t in range(halves):
        grads = grad_mixed[t]
        if t == 0:
            grads = tie(grads, grad_mixed, grad_proj)
        else:
            grads = tie(grads, fc1_sum.far, fc2_sum.result)
        grad_proj_in, column_sums = attention_backward(*kept[t], grads)
        column_sums = jnp.sum(column_sums, axis=0)
        grad_proj_ins.append(grad_proj_in)
        grad_front.append(
            [low(transpose_dot(normed_low, grad_proj_in)), grad_proj[t]]
        )
        grad_query_bias.append(
            jnp.stack([column_sums[:shard_width], column_sums[2 * shard_width :]])
        )
        if t == 0:
            fc1_sum.far = tie_all(fc1_sum.far, grad_proj_in)
            fc1_sum.send_near()
        else:
            fc1_sum.near = tie(fc1_sum.near, grad_proj_in)
            fc1_sum.send_deep()
    front_sum = Scatter(ring, grad_front)
    front_sum.send_core()
    activated = [tie(a, front_sum.sent) for a in activated]
    ffn_out = norm_bias[5]
    for t in range(halves):
        ffn_out = ffn_out + dot_back(activated[t], fc2_low[t])
    block_out = low(hidden_res + ffn_out)
    front_sum.arrived = tie_all(front_sum.arrived, block_out)
    front_sum.send_far()
    grad_normed = 0.0
    for t in range(halves):
        grad_normed = grad_normed + dot_back(
            tie(grad_proj_ins[t], front_sum.arrived), qkv_low[t]
        )
    front_sum.far = tie_all(front_sum.far, grad_normed)
    front_sum.send_near()
    grad_normed = tie(grad_normed, front_sum.far)
    front_sum.send_deep()
    front_shard, fc1_shard, fc2_shard = front_sum.result, fc1_sum.result, fc2_sum.result
    grad_input_norm, grad_gain_one, grad_shift_one = norm_back(grad_normed)
    input_grad = grad_hidden + grad_input_norm
    grad_split = jnp.concatenate(
        [
            jnp.concatenate([grad_query_bias[t], grad_fc1_bias[t]])
            for t in range(halves)
        ],
        axis=1,
    )
    grad_norm_rows = jnp.stack(
        [
            grad_gain_one,
            grad_shift_one,
            jnp.sum(wide(grad_attn_low), axis=0),
            grad_gain_two,
            grad_shift_two,
            jnp.sum(grad_out, axis=0),
        ]
    )
    shards = (
        front_shard[:, : 3 * shard_width].reshape(shard_rows, 3, shard_width),
        rows_of(front_shard[:, 3 * shard_width :]),
        fc1_shard.reshape(shard_rows, 4, shard_width),
        jnp.transpose(fc2_shard.reshape(shard_rows, 4, shard_width), (1, 2, 0)),
    )
    local_square = square_sum((front_shard, fc1_shard, fc2_shard))
    vectors = jnp.concatenate(
        [grad_norm_rows, grad_split, jnp.full((4, model_width), local_square)]
    )
    vectors = sum_everywhere(ring, vectors)
    norm_total, split_whole, square_total = vectors[:6], vectors[6:12], vectors[12, 0]
    vectors = vectors[:12]
    split_total = jnp.where(
        ring.across == 0, split_whole[:, :shard_width], split_whole[:, shard_width:]
    )
    grad_norm = jnp.sqrt(square_total + jnp.sum(vectors * vectors))
    factor = jnp.minimum(1.0, clip_value / (grad_norm + 1e-06))
    step_value = step_count[0].astype(jnp.float32)
    bias_first = 1.0 - jnp.power(beta_one, step_value)
    bias_second = 1.0 - jnp.power(beta_two, step_value)
    qkv_out = adam_update(
        w_qkv, shards[0], m_qkv, v_qkv, factor, bias_first, bias_second, matrix_rate, matrix_decay
    )
    proj_out = adam_update(
        w_proj, shards[1], m_proj, v_proj, factor, bias_first, bias_second, proj_rate, matrix_decay
    )
    fc1_out = adam_update(
        w_fc1, shards[2], m_fc1, v_fc1, factor, bias_first, bias_second, matrix_rate, matrix_decay
    )
    fc2_out = adam_update(
        w_fc2, shards[3], m_fc2, v_fc2, factor, bias_first, bias_second, matrix_rate, matrix_decay
    )
    split_out = adam_update(
        split_bias, split_total, m_split, v_split, factor, bias_first, bias_second, vector_rate, 0.0
    )
    norm_out = adam_update(
        norm_bias, norm_total, m_norm, v_norm, factor, bias_first, bias_second, vector_rate, 0.0
    )
    return (
        block_out,
        input_grad,
        grad_norm,
        qkv_out[0],
        qkv_out[1],
        qkv_out[2],
        proj_out[0],
        proj_out[1],
        proj_out[2],
        fc1_out[0],
        fc1_out[1],
        fc1_out[2],
        fc2_out[0],
        fc2_out[1],
        fc2_out[2],
        split_out[0],
        split_out[1],
        split_out[2],
        norm_out[0],
        norm_out[1],
        norm_out[2],
    )


def solution(mesh):
    sizes = (mesh.shape["dp"], mesh.shape["tensor"])
    return jax.shard_map(
        partial(body, sizes),
        mesh=mesh,
        in_specs=(
            P(("dp", "tensor"), None),
            P(("dp", "tensor"), None),
            P(),
            P(("dp", "tensor"), None),
            P(),
            P("dp", None, "tensor"),
            P("dp", None, "tensor"),
            P("dp", None, "tensor"),
            P("tensor", "dp"),
            P("tensor", "dp"),
            P("tensor", "dp"),
            P("dp", None, "tensor"),
            P("dp", None, "tensor"),
            P("dp", None, "tensor"),
            P(None, "tensor", "dp"),
            P(None, "tensor", "dp"),
            P(None, "tensor", "dp"),
            P(None, "tensor"),
            P(None, "tensor"),
            P(None, "tensor"),
            P(),
            P(),
            P(),
        ),
        out_specs=(
            P(("dp", "tensor"), None),
            P(("dp", "tensor"), None),
            P(),
            P("dp", None, "tensor"),
            P("dp", None, "tensor"),
            P("dp", None, "tensor"),
            P("tensor", "dp"),
            P("tensor", "dp"),
            P("tensor", "dp"),
            P("dp", None, "tensor"),
            P("dp", None, "tensor"),
            P("dp", None, "tensor"),
            P(None, "tensor", "dp"),
            P(None, "tensor", "dp"),
            P(None, "tensor", "dp"),
            P(None, "tensor"),
            P(None, "tensor"),
            P(None, "tensor"),
            P(),
            P(),
            P(),
        ),
        check_vma=False,
    )
```

```python
from functools import partial

import jax
import jax.numpy as jnp
import numpy as np
from jax import lax
from jax.experimental import pallas as pl
from jax.experimental.pallas import tpu as pltpu
from jax.sharding import PartitionSpec as P

HD = 64
VISIBLE = 49


norm_eps = 1e-06
beta_one = 0.9
beta_two = 0.95
adam_eps = 1e-08
clip_value = 1.0
matrix_rate = 0.02
proj_rate = 0.08
vector_rate = 0.2
matrix_decay = 0.05


def layer_norm(values, row_gain, row_shift):
    row_mean = jnp.mean(values, axis=-1, keepdims=True)
    centred = values - row_mean
    variance = jnp.mean(centred * centred, axis=-1, keepdims=True)
    return centred * lax.rsqrt(variance + norm_eps) * row_gain + row_shift


def adam_update(
    weight, gradient, first_moment, second, factor, bias_first, bias_second, learn_rate, decay_rate
):
    clipped = gradient * factor
    first_new = beta_one * first_moment + (1.0 - beta_one) * clipped
    second_new = beta_two * second + (1.0 - beta_two) * clipped * clipped
    direction = first_new / bias_first / (jnp.sqrt(second_new / bias_second) + adam_eps)
    return (weight - learn_rate * (direction + decay_rate * weight), first_new, second_new)


def transpose_dot(left_side, right_side):
    return lax.dot_general(
        left_side, right_side, (((0,), (0,)), ((), ())), preferred_element_type=jnp.float32
    )


def dot_back(left_side, right_side):
    return lax.dot_general(
        left_side, right_side, (((1,), (1,)), ((), ())), preferred_element_type=jnp.float32
    )


def square_sum(arrays):
    total = jnp.sum(arrays[0] * arrays[0])
    for member in arrays[1:]:
        total = total + jnp.sum(member * member)
    return total


def standard_normal(values):
    cumulative = 0.5 + 0.5 * lax.erf(values * (0.5**0.5))
    density = jnp.exp(-0.5 * values * values) * (0.5 / jnp.pi) ** 0.5
    return cumulative, density


every_axis = ("dp", "tensor")
low_type = jnp.bfloat16
wide_type = jnp.float32
WINDOW_IMAGES = 2
QUERY_ROWS = 112
KEY_ROWS = 128
PAIR = 2 * HD
GROUP_IMAGES = 16
GROUP_ROWS = GROUP_IMAGES * VISIBLE
WINDOWS = GROUP_IMAGES // WINDOW_IMAGES
WINDOW_UNROLL = 8
HIDDEN = -1e30


def wide(values):
    return values.astype(wide_type)


class Exchange:
    def __init__(self, dp_size, tensor_size):
        self.total = dp_size * tensor_size
        self.outer = self.total // 8
        flat_dp = lax.axis_index("dp")
        self.across = lax.axis_index("tensor")
        self.core = flat_dp & 1
        self.up = (flat_dp >> 1) & 1
        self.deep = flat_dp >> 2

    def swap(self, value, mask):
        return lax.ppermute(value, every_axis, [(i, i ^ mask) for i in range(self.total)])

    def swap_by_core(self, value, even_mask, odd_mask):
        masks = (even_mask, odd_mask)
        return lax.ppermute(
            value, every_axis, [(i, i ^ masks[(i >> 1) & 1]) for i in range(self.total)]
        )

    def digits(self):
        size = 1
        while size < self.outer:
            radix = 4 if self.outer // size >= 4 else 2
            yield size, radix
            size *= radix

    def spot(self, core, flip_second, flip_first):
        first = jnp.where(core == 0, self.up, self.across) ^ flip_first
        second = jnp.where(core == 0, self.across, self.up) ^ flip_second
        return jnp.where(core == 0, second, first), jnp.where(core == 0, first, second)


def tie(value, *others):
    return lax.optimization_barrier((value,) + tuple(jax.tree.leaves(others)))[0]


def tie_all(values, *others):
    leaves = tuple(jax.tree.leaves(others))
    return list(lax.optimization_barrier(tuple(values) + leaves)[: len(values)])


def deposit(pieces, slots):
    count = len(pieces)
    shape = (count,) + pieces[0].shape

    def kernel(spots, *refs):
        out, done = refs[count], refs[count + 1]
        copies = [
            pltpu.make_async_copy(refs[k], out.at[spots[k]], done.at[k]) for k in range(count)
        ]
        for copy in copies:
            copy.start()
        for copy in copies:
            copy.wait()

    return pl.pallas_call(
        kernel,
        out_shape=jax.ShapeDtypeStruct(shape, pieces[0].dtype),
        grid_spec=pltpu.PrefetchScalarGridSpec(
            num_scalar_prefetch=1,
            grid=(1,),
            in_specs=[pl.BlockSpec(memory_space=pl.ANY)] * count,
            out_specs=pl.BlockSpec(
                shape, lambda i, spots: (0,) * len(shape), pipeline_mode=pl.Buffered(1)
            ),
            scratch_shapes=[pltpu.SemaphoreType.DMA((count,))],
        ),
        name="deposit",
    )(jnp.stack(slots).astype(jnp.int32), *pieces)


def deposit_whole(pieces, slots, widths):
    count = len(pieces)
    outer, rows, _ = pieces[0].shape
    starts = [sum(widths[:w]) for w in range(len(widths))]

    def kernel(spots, *refs):
        out, done = refs[count : count + len(widths)], refs[-1]
        copies = []
        for k in range(count):
            for w, width in enumerate(widths):
                cols = pl.ds(pl.multiple_of(spots[3 * k] * width, 128), width)
                source = refs[k].at[:, :, pl.ds(starts[w], width)]
                target = out[w].at[:, spots[3 * k + 1], spots[3 * k + 2], :, cols]
                copies.append(pltpu.make_async_copy(source, target, done.at[k, w]))
        for copy in copies:
            copy.start()
        for copy in copies:
            copy.wait()

    shapes = [(outer, 2, 2, rows, 2 * width) for width in widths]
    flat = jnp.stack([jnp.asarray(v, jnp.int32) for slot in slots for v in slot])
    whole = pl.pallas_call(
        kernel,
        out_shape=[jax.ShapeDtypeStruct(shape, low_type) for shape in shapes],
        grid_spec=pltpu.PrefetchScalarGridSpec(
            num_scalar_prefetch=1,
            grid=(1,),
            in_specs=[pl.BlockSpec(memory_space=pl.ANY)] * count,
            out_specs=[
                pl.BlockSpec(shape, lambda i, spots: (0,) * 5, pipeline_mode=pl.Buffered(1))
                for shape in shapes
            ],
            scratch_shapes=[pltpu.SemaphoreType.DMA((count, len(widths)))],
        ),
        name="deposit_whole",
    )(flat, *pieces)
    return [part.reshape(outer * 4 * rows, part.shape[-1]) for part in whole]


class Gather:
    def __init__(self, ring, name, block, widths):
        self.ring, self.name = ring, name
        self.cur, self.widths = block[None], widths

    def send_deep(self):
        with jax.named_scope(self.name + "_deep"):
            ring = self.ring
            steps = list(ring.digits())
            for size, radix in steps:
                self.spot = (ring.deep // size) % radix
                self.arrived = [ring.swap(self.cur, (k * size) << 3) for k in range(1, radix)]
                if (size, radix) != steps[-1]:
                    self.collect()

    def collect(self):
        with jax.named_scope(self.name + "_collect"):
            radix = 1 + len(self.arrived)
            stacked = deposit([self.cur] + self.arrived, [self.spot ^ k for k in range(radix)])
            self.cur = stacked.reshape((radix * self.cur.shape[0],) + self.cur.shape[1:])

    def send_beside(self):
        with jax.named_scope(self.name + "_beside"):
            self.collect()
            self.beside = self.ring.swap_by_core(self.cur, 4, 1)

    def send_far(self):
        ring, mine = self.ring, [self.cur, self.beside]
        with jax.named_scope(self.name + "_far"):
            self.far = [ring.swap_by_core(piece, 1, 4) for piece in mine]
        with jax.named_scope(self.name + "_core"):
            self.early = [ring.swap(piece, 2) for piece in mine]

    def send_core(self):
        self.mine = [self.cur, self.beside] + self.far
        with jax.named_scope(self.name + "_core"):
            self.theirs = self.early + [self.ring.swap(piece, 2) for piece in self.far]

    def whole(self):
        with jax.named_scope(self.name + "_whole"):
            ring = self.ring
            slots = []
            for core in (ring.core, 1 - ring.core):
                for flip_second in range(2):
                    for flip_first in range(2):
                        slots.append(ring.spot(core, flip_second, flip_first) + (core,))
            return deposit_whole(self.mine + self.theirs, slots, self.widths)


class Scatter:
    def __init__(self, ring, name, parts):
        self.ring, self.name = ring, name
        self.rows = parts[0].shape[0] // (ring.outer * 4)
        shape = (ring.outer, 2, 2, self.rows)
        self.views = [part.reshape(shape + part.shape[1:]) for part in parts]

    def cut(self, t, core, up=None):
        cuts = []
        for view in self.views:
            ups, width = 2 if up is None else 1, view.shape[4] // 2
            part = lax.dynamic_slice(
                view[..., t * width : (t + 1) * width],
                (0, 0 if up is None else up, core, 0, 0),
                (view.shape[0], ups, 1, view.shape[3], width),
            )
            cuts.append(part.reshape(view.shape[0], ups, view.shape[3], width))
        return cuts[0] if len(cuts) == 1 else jnp.concatenate(cuts, axis=-1)

    def send_core(self):
        with jax.named_scope(self.name + "_core"):
            self.sent = [self.cut(t, 1 - self.ring.core) for t in range(2)]
            self.arrived = [self.ring.swap(part, 2) for part in self.sent]

    def partial(self, flip_second, flip_first):
        across, up = self.ring.spot(self.ring.core, flip_second, flip_first)
        terms = [
            wide(self.cut(t, self.ring.core, up)[:, 0])
            + wide(lax.dynamic_index_in_dim(self.arrived[t], up, 1, keepdims=False))
            for t in range(2)
        ]
        return jnp.where(across == 0, terms[0], terms[1])

    def send_far(self):
        swap = self.ring.swap_by_core
        with jax.named_scope(self.name + "_far"):
            self.sent = [self.partial(1, k).astype(low_type) for k in (1, 0)]
            self.far = [swap(part, 1, 4) for part in self.sent]

    def send_near(self):
        with jax.named_scope(self.name + "_near"):
            self.sent = (self.partial(0, 1) + wide(self.far[0])).astype(low_type)
            self.near = self.ring.swap_by_core(self.sent, 4, 1)

    def send_deep(self):
        ring = self.ring
        with jax.named_scope(self.name + "_deep"):
            self.cur = self.partial(0, 0) + wide(self.far[1]) + wide(self.near)
            steps = list(reversed(list(ring.digits())))
            for size, radix in steps:
                spot = (ring.deep // size) % radix
                cur = self.cur.reshape((radix, size) + self.cur.shape[-2:])
                cut = partial(lax.dynamic_index_in_dim, axis=0, keepdims=False)
                self.sent = [cut(cur, spot ^ k).astype(low_type) for k in range(1, radix)]
                self.deep = [
                    ring.swap(part, (k * size) << 3) for k, part in enumerate(self.sent, 1)
                ]
                self.cur = cut(cur, spot)
                if (size, radix) != steps[-1]:
                    self.collect()

    def collect(self):
        for part in self.deep:
            self.cur = self.cur + wide(part)

    def finish(self):
        self.collect()
        return self.cur.reshape(self.cur.shape[1:])


def sum_everywhere(ring, value):
    bit = 1
    while bit < ring.total:
        radix = 4 if ring.total // bit >= 4 else 2
        terms = [value] + [ring.swap(value, k * bit) for k in range(1, radix)]
        while len(terms) > 1:
            terms = [terms[i] + terms[i + 1] for i in range(0, len(terms), 2)]
        value = terms[0]
        bit *= radix
    return value


def window_rows(index):
    query_start = (index * (WINDOW_IMAGES * VISIBLE)) // 16 * 16
    key_start = jnp.minimum(query_start, GROUP_ROWS - KEY_ROWS)
    return (
        pl.ds(pl.multiple_of(query_start, 16), QUERY_ROWS),
        pl.ds(pl.multiple_of(key_start, 16), KEY_ROWS),
    )


def window_masks():
    base = np.arange(WINDOWS)[:, None, None] * (WINDOW_IMAGES * VISIBLE)
    query_start = base // 16 * 16
    key_start = np.minimum(query_start, GROUP_ROWS - KEY_ROWS)
    query_at = query_start - base + np.arange(QUERY_ROWS)[None, :, None]
    key_at = key_start - base + np.arange(KEY_ROWS)[None, None, :]
    used = (query_at >= 0) & (query_at < WINDOW_IMAGES * VISIBLE)
    low_key = np.where(query_at < VISIBLE, 0, VISIBLE)
    allowed = used & (key_at >= low_key) & (key_at < low_key + VISIBLE)
    return np.where(allowed, 0.0, HIDDEN).astype(np.float32)


def split_pair(values):
    lane = lax.broadcasted_iota(jnp.int32, values.shape, 1)
    zero = jnp.zeros_like(values)
    return jnp.concatenate(
        [jnp.where(lane < HD, values, zero), jnp.where(lane >= HD, values, zero)], axis=0
    )


def join_pair(stacked):
    lane = lax.broadcasted_iota(jnp.int32, (KEY_ROWS, PAIR), 1)
    return jnp.where(lane < HD, stacked[:KEY_ROWS], stacked[KEY_ROWS:])


def over_windows(window, store):
    def several(step, carry):
        places = [step * WINDOW_UNROLL + offset for offset in range(WINDOW_UNROLL)]
        results = [window(place) for place in places]
        for place, result in zip(places, results):
            store(place, *result)
        return carry

    lax.fori_loop(0, WINDOWS // WINDOW_UNROLL, several, 0)


def head_blocks(shape, head_axis, value):
    own_axis = 1 - head_axis
    lanes = lax.broadcasted_iota(jnp.int32, shape, head_axis) < HD
    stack = lax.broadcasted_iota(jnp.int32, shape, own_axis) < KEY_ROWS
    return jnp.where(lanes == stack, value, 0.0).astype(low_type)


def attention_forward_kernel(queries, keys, values, hide, *refs):
    mixed, soft, scale = refs[-3:]
    mixed[...] = jnp.zeros_like(mixed)
    ones = head_blocks((2 * KEY_ROWS, PAIR), 1, 1.0)

    def window(index):
        query_rows, key_rows = window_rows(index)
        scaled = queries[query_rows, :] * jnp.asarray(HD**-0.5, low_type)
        scores = dot_back(scaled, split_pair(keys[key_rows, :]))
        weights = []
        for head in range(2):
            part = scores[:, head * KEY_ROWS : (head + 1) * KEY_ROWS] + hide[index]
            highest = jnp.maximum(jnp.max(part, axis=-1, keepdims=True), HIDDEN / 4)
            weights.append(jnp.exp(part - highest).astype(low_type))
        weights = jnp.concatenate(weights, axis=1)
        right = jnp.concatenate([split_pair(values[key_rows, :]), ones], axis=1)
        result = jnp.dot(weights, right, preferred_element_type=wide_type)
        total = result[:, PAIR:]
        inverse = jnp.where(total > 0.0, 1.0 / total, 0.0)
        return weights, inverse, (result[:, :PAIR] * inverse).astype(low_type)

    def store(index, weights, inverse, result):
        soft[index, 0] = weights
        scale[index, 0] = inverse
        mixed[window_rows(index)[0], :] += result

    over_windows(window, store)


def attention_backward_kernel(
    queries, keys, values, soft, scale, mixed, grad_mixed, *refs, width
):
    grad_qkv, sums = refs[-2:]
    pairs = width // PAIR
    first_col = pl.program_id(0) // pairs * (3 * width) + pl.program_id(0) % pairs * PAIR
    query_cols, key_cols, value_cols = [
        pl.ds(pl.multiple_of(first_col + part * width, PAIR), PAIR) for part in range(3)
    ]
    minus_ones = head_blocks((2 * KEY_ROWS, PAIR), 1, -1.0)
    for cols in (query_cols, key_cols, value_cols):
        grad_qkv[:, cols] = jnp.zeros((GROUP_ROWS, PAIR), low_type)
        sums[:, cols] = jnp.zeros((8, PAIR), wide_type)

    def window(index):
        query_rows, key_rows = window_rows(index)
        split_keys = split_pair(keys[key_rows, :])
        weights = soft[index, 0]
        grads = wide(grad_mixed[query_rows, :]) * scale[index, 0]
        shares = (grads * wide(mixed[query_rows, :])).astype(low_type)
        grads = grads.astype(low_type)
        left = jnp.concatenate([grads, shares], axis=1)
        right = jnp.concatenate([split_pair(values[key_rows, :]), minus_ones], axis=1)
        grad_scores = (wide(weights) * dot_back(left, right)).astype(low_type)
        grad_queries = (
            jnp.dot(grad_scores, split_keys, preferred_element_type=wide_type) * HD**-0.5
        )
        grad_keys = join_pair(transpose_dot(grad_scores, queries[query_rows, :])) * HD**-0.5
        grad_values = join_pair(transpose_dot(weights, grads))
        return (
            grad_queries.astype(low_type),
            grad_keys.astype(low_type),
            grad_values.astype(low_type),
            jnp.sum(grad_queries.reshape(-1, 8, PAIR), axis=0),
            jnp.sum(grad_values.reshape(-1, 8, PAIR), axis=0),
        )

    def store(index, grad_queries, grad_keys, grad_values, query_sums, value_sums):
        query_rows, key_rows = window_rows(index)
        grad_qkv[query_rows, query_cols] += grad_queries
        grad_qkv[key_rows, key_cols] += grad_keys
        grad_qkv[key_rows, value_cols] += grad_values
        sums[:, query_cols] += query_sums
        sums[:, value_cols] += value_sums

    over_windows(window, store)


def pair_blocks(pairs, of_group, of_pair):
    return [
        pl.BlockSpec(
            (GROUP_ROWS, PAIR),
            lambda p, k=k: (of_group, of_pair(p) // pairs * 3 * pairs + k * pairs + of_pair(p) % pairs),
        )
        for k in range(3)
    ]


def attention_forward(qkv, width, group, half, before=()):
    rows, all_width = qkv.shape[0], qkv.shape[1] // 3
    pairs, all_pairs = width // PAIR, all_width // PAIR
    hide = window_masks()
    of_pair = lambda p: half * pairs + p
    window_block = lambda p: (group, of_pair(p), 0, 0)
    return pl.pallas_call(
        attention_forward_kernel,
        grid=(pairs,),
        in_specs=pair_blocks(pairs, group, of_pair)
        + [pl.BlockSpec(hide.shape, lambda p: (0, 0, 0), pipeline_mode=pl.Buffered(1))]
        + [pl.BlockSpec(memory_space=pl.ANY)] * len(before),
        out_specs=[
            pl.BlockSpec((GROUP_ROWS, PAIR), lambda p: (group, of_pair(p))),
            pl.BlockSpec((WINDOWS, 1, QUERY_ROWS, 2 * KEY_ROWS), window_block),
            pl.BlockSpec((WINDOWS, 1, QUERY_ROWS, PAIR), window_block),
        ],
        out_shape=[
            jax.ShapeDtypeStruct((rows, all_width), low_type),
            jax.ShapeDtypeStruct(
                (rows // GROUP_ROWS * WINDOWS, all_pairs, QUERY_ROWS, 2 * KEY_ROWS), low_type
            ),
            jax.ShapeDtypeStruct(
                (rows // GROUP_ROWS * WINDOWS, all_pairs, QUERY_ROWS, PAIR), wide_type
            ),
        ],
        input_output_aliases={4 + k: k for k in range(len(before))},
        name="attention_forward",
    )(qkv, qkv, qkv, hide, *before)


def attention_backward(qkv, mixed, soft, scale, grad_mixed, width, group, before=()):
    rows, all_width = qkv.shape[0], qkv.shape[1] // 3
    pairs, all_pairs = width // PAIR, all_width // PAIR
    window_block = lambda p: (group, p, 0, 0)
    row_block = pl.BlockSpec((GROUP_ROWS, PAIR), lambda p: (group, p))
    return pl.pallas_call(
        partial(attention_backward_kernel, width=width),
        grid=(all_pairs,),
        in_specs=pair_blocks(pairs, group, lambda p: p)
        + [
            pl.BlockSpec((WINDOWS, 1, QUERY_ROWS, 2 * KEY_ROWS), window_block),
            pl.BlockSpec((WINDOWS, 1, QUERY_ROWS, PAIR), window_block),
            row_block,
            row_block,
        ]
        + [pl.BlockSpec(memory_space=pl.ANY)] * len(before),
        out_specs=[
            pl.BlockSpec((GROUP_ROWS, 3 * all_width), lambda p: (group, 0)),
            pl.BlockSpec((8, 3 * all_width), lambda p: (0, 0)),
        ],
        out_shape=[
            jax.ShapeDtypeStruct((rows, 3 * all_width), low_type),
            jax.ShapeDtypeStruct((8, 3 * all_width), wide_type),
        ],
        input_output_aliases={7: 0} if before else {},
        name="attention_backward",
    )(qkv, qkv, qkv, soft, scale, mixed, grad_mixed, *before)


def body(
    sizes,
    patches,
    visible,
    pos_table,
    cotangent,
    step_count,
    w_qkv,
    m_qkv,
    v_qkv,
    w_proj,
    m_proj,
    v_proj,
    w_fc1,
    m_fc1,
    v_fc1,
    w_fc2,
    m_fc2,
    v_fc2,
    split_bias,
    m_split,
    v_split,
    norm_bias,
    m_norm,
    v_norm,
):
    model_width = patches.shape[1]
    full_rows = patches.shape[0]
    shard_rows = w_qkv.shape[0]
    shard_width = w_qkv.shape[2]
    ring = Exchange(*sizes)

    def rows_of(proj_like):
        return jnp.swapaxes(proj_like, -1, -2)

    def low(block):
        return block.astype(low_type)

    mid_block = jnp.concatenate(
        [rows_of(w_proj), w_fc1.reshape(shard_rows, 4 * shard_width)], axis=1
    )
    fc2_block = jnp.transpose(w_fc2, (2, 0, 1)).reshape(shard_rows, 4 * shard_width)
    qkv_block = low(w_qkv.reshape(shard_rows, 3 * shard_width))
    qkv_all = Gather(ring, "qkv", qkv_block, [3 * shard_width])
    qkv_all.send_deep()
    qkv_all.send_beside()
    mid_all = Gather(
        ring, "mid", tie(low(mid_block), qkv_all.cur), [shard_width, 4 * shard_width]
    )
    mid_all.send_deep()
    qkv_all.send_far()
    qkv_all.send_core()
    fc2_all = Gather(ring, "fc2", tie(low(fc2_block), qkv_all.far), [4 * shard_width])
    fc2_all.send_deep()
    (qkv_low,) = qkv_all.whole()
    mid_all.arrived = tie_all(mid_all.arrived, qkv_low)
    mid_all.send_beside()
    other_bias = ring.swap(tie(split_bias, qkv_all.cur), 1)
    bias_halves = [jnp.where(ring.across == t, split_bias, other_bias) for t in range(2)]
    zero_bias = jnp.zeros((shard_width,), wide_type)
    qkv_shift = jnp.concatenate([v for b in bias_halves for v in (b[0], zero_bias, b[1])])
    fc1_shift = jnp.concatenate([b[2:].reshape(-1) for b in bias_halves])

    places = tie(visible, qkv_all.cur).reshape(-1)
    inputs = wide(patches) + jnp.take(pos_table, places, axis=0)
    normed, norm_back = jax.vjp(layer_norm, inputs, norm_bias[0], norm_bias[1])
    normed_low = low(normed)
    left = tie(normed_low, mid_all.cur)
    projected = low(jnp.dot(left, qkv_low, preferred_element_type=wide_type) + qkv_shift)
    groups = full_rows // GROUP_ROWS
    outcome = ()
    for call in range(2 * groups):
        outcome = attention_forward(projected, shard_width, call // 2, call % 2, outcome)
        if call == 0:
            mid_all.beside = tie(mid_all.beside, outcome)
            mid_all.send_far()
        if call == 2 * groups - 1:
            mid_all.far = tie_all(mid_all.far, outcome)
            mid_all.send_core()
            fc2_all.arrived = tie_all(fc2_all.arrived, outcome)
            fc2_all.send_beside()
    mixed_low, soft_low, soft_scale = outcome
    mid_all.theirs = tie_all(mid_all.theirs, mixed_low)
    proj_low, fc1_low = mid_all.whole()
    attended = dot_back(mixed_low, proj_low)
    fc2_all.beside = tie(fc2_all.beside, attended)
    fc2_all.send_far()
    hidden_res = inputs + (attended + norm_bias[2])
    normed_two, norm_two_back = jax.vjp(layer_norm, hidden_res, norm_bias[3], norm_bias[4])
    normed_two_low = low(normed_two)
    grad_out = wide(cotangent)
    pre_gelu = jnp.dot(normed_two_low, fc1_low, preferred_element_type=wide_type) + fc1_shift
    cumulative, density = standard_normal(pre_gelu)
    activated = low(pre_gelu * cumulative)
    slope = low(cumulative + pre_gelu * density)
    fc2_all.far = tie_all(fc2_all.far, activated)
    fc2_all.send_core()
    grad_fc2 = low(transpose_dot(cotangent, activated))
    fc2_all.theirs = tie_all(fc2_all.theirs, grad_fc2)
    (fc2_low,) = fc2_all.whole()
    fc2_sum = Scatter(ring, "fc2_sum", [grad_fc2])
    fc2_sum.send_core()
    cotangent_later = tie(cotangent, fc2_sum.sent)
    grad_act = jnp.dot(cotangent_later, fc2_low, preferred_element_type=wide_type)
    grad_pre = low(grad_act * wide(slope))
    grad_fc1_bias = jnp.sum(wide(grad_pre), axis=0)
    fc2_sum.arrived = tie_all(fc2_sum.arrived, grad_pre)
    fc2_sum.send_far()
    grad_fc1 = low(transpose_dot(normed_two_low, tie(grad_pre, fc2_sum.arrived)))
    fc1_sum = Scatter(ring, "fc1_sum", [grad_fc1])
    fc1_sum.send_core()
    fc2_sum.far = tie_all(fc2_sum.far, grad_fc1)
    fc2_sum.send_near()
    grad_normed_two = dot_back(tie(grad_pre, fc1_sum.sent, fc2_sum.far), fc1_low)
    fc2_sum.near = tie(fc2_sum.near, grad_normed_two)
    fc2_sum.send_deep()
    fc1_sum.arrived = tie_all(fc1_sum.arrived, grad_normed_two)
    fc1_sum.send_far()
    grad_hidden_norm, grad_gain_two, grad_shift_two = norm_two_back(
        tie(grad_normed_two, fc1_sum.arrived, fc2_sum.near)
    )
    grad_hidden = grad_out + grad_hidden_norm
    grad_attn_low = low(grad_hidden)
    grad_proj = low(transpose_dot(grad_attn_low, mixed_low))
    grad_mixed = low(jnp.dot(grad_attn_low, proj_low, preferred_element_type=wide_type))
    fc2_shard = fc2_sum.finish()
    gradient, column_sums = (), 0.0
    for group in range(groups):
        if group == 0:
            source = tie(grad_mixed, grad_proj)
        else:
            source = tie(grad_mixed, fc1_sum.sent)
        *gradient, sums = attention_backward(
            projected, mixed_low, soft_low, soft_scale, source, shard_width, group, gradient
        )
        column_sums = column_sums + jnp.sum(sums, axis=0)
        if group == 0:
            fc1_sum.far = tie_all(fc1_sum.far, gradient)
            fc1_sum.send_near()
        elif group == groups - 1:
            fc1_sum.near = tie(fc1_sum.near, gradient)
            fc1_sum.send_deep()
    (grad_projected,) = gradient
    grad_qkv = low(transpose_dot(normed_low, grad_projected))
    front_sum = Scatter(ring, "front_sum", [grad_qkv, grad_proj])
    front_sum.send_core()
    out_column_sums = jnp.stack(
        [
            jnp.sum(wide(values), axis=0)
            for values in tie_all([grad_attn_low, cotangent], front_sum.sent)
        ]
    )
    front_sum.arrived = tie_all(front_sum.arrived, out_column_sums)
    front_sum.send_far()
    ffn_out = dot_back(tie(activated, front_sum.sent), fc2_low) + norm_bias[5]
    block_out = low(hidden_res + ffn_out)
    front_sum.far = tie_all(front_sum.far, block_out)
    front_sum.send_near()
    grad_normed = dot_back(tie(grad_projected, front_sum.sent), qkv_low)
    front_sum.near = tie(front_sum.near, grad_normed)
    front_sum.send_deep()
    grad_normed = tie(grad_normed, front_sum.sent)
    fc1_sum.deep = tie_all(fc1_sum.deep, grad_normed)
    fc1_shard = fc1_sum.finish()
    grad_input_norm, grad_gain_one, grad_shift_one = norm_back(grad_normed)
    input_grad = grad_hidden + grad_input_norm
    column_sums = column_sums.reshape(2, 3, shard_width)
    grad_split = jnp.concatenate(
        [
            column_sums[:, 0].reshape(1, -1),
            column_sums[:, 2].reshape(1, -1),
            jnp.swapaxes(grad_fc1_bias.reshape(2, 4, shard_width), 0, 1).reshape(4, -1),
        ]
    )
    grad_norm_rows = jnp.stack(
        [
            grad_gain_one,
            grad_shift_one,
            out_column_sums[0],
            grad_gain_two,
            grad_shift_two,
            out_column_sums[1],
        ]
    )
    front_sum.deep = tie_all(front_sum.deep, input_grad, grad_norm_rows)
    front_shard = front_sum.finish()
    shards = (
        front_shard[:, : 3 * shard_width].reshape(shard_rows, 3, shard_width),
        rows_of(front_shard[:, 3 * shard_width :]),
        fc1_shard.reshape(shard_rows, 4, shard_width),
        jnp.transpose(fc2_shard.reshape(shard_rows, 4, shard_width), (1, 2, 0)),
    )
    local_square = square_sum((front_shard, fc1_shard, fc2_shard))
    vectors = jnp.concatenate(
        [grad_norm_rows, grad_split, jnp.full((4, model_width), local_square)]
    )
    vectors = sum_everywhere(ring, vectors)
    norm_total, split_whole, square_total = vectors[:6], vectors[6:12], vectors[12, 0]
    vectors = vectors[:12]
    split_total = jnp.where(
        ring.across == 0, split_whole[:, :shard_width], split_whole[:, shard_width:]
    )
    grad_norm = jnp.sqrt(square_total + jnp.sum(vectors * vectors))
    factor = jnp.minimum(1.0, clip_value / (grad_norm + 1e-06))
    step_value = step_count[0].astype(jnp.float32)
    bias_first = 1.0 - jnp.power(beta_one, step_value)
    bias_second = 1.0 - jnp.power(beta_two, step_value)
    qkv_out = adam_update(
        w_qkv, shards[0], m_qkv, v_qkv, factor, bias_first, bias_second, matrix_rate, matrix_decay
    )
    proj_out = adam_update(
        w_proj, shards[1], m_proj, v_proj, factor, bias_first, bias_second, proj_rate, matrix_decay
    )
    fc1_out = adam_update(
        w_fc1, shards[2], m_fc1, v_fc1, factor, bias_first, bias_second, matrix_rate, matrix_decay
    )
    fc2_out = adam_update(
        w_fc2, shards[3], m_fc2, v_fc2, factor, bias_first, bias_second, matrix_rate, matrix_decay
    )
    split_out = adam_update(
        split_bias, split_total, m_split, v_split, factor, bias_first, bias_second, vector_rate, 0.0
    )
    norm_out = adam_update(
        norm_bias, norm_total, m_norm, v_norm, factor, bias_first, bias_second, vector_rate, 0.0
    )
    return (
        block_out,
        input_grad,
        grad_norm,
        qkv_out[0],
        qkv_out[1],
        qkv_out[2],
        proj_out[0],
        proj_out[1],
        proj_out[2],
        fc1_out[0],
        fc1_out[1],
        fc1_out[2],
        fc2_out[0],
        fc2_out[1],
        fc2_out[2],
        split_out[0],
        split_out[1],
        split_out[2],
        norm_out[0],
        norm_out[1],
        norm_out[2],
    )


def solution(mesh):
    sizes = (mesh.shape["dp"], mesh.shape["tensor"])
    return jax.shard_map(
        partial(body, sizes),
        mesh=mesh,
        in_specs=(
            P(("dp", "tensor"), None),
            P(("dp", "tensor"), None),
            P(),
            P(("dp", "tensor"), None),
            P(),
            P("dp", None, "tensor"),
            P("dp", None, "tensor"),
            P("dp", None, "tensor"),
            P("tensor", "dp"),
            P("tensor", "dp"),
            P("tensor", "dp"),
            P("dp", None, "tensor"),
            P("dp", None, "tensor"),
            P("dp", None, "tensor"),
            P(None, "tensor", "dp"),
            P(None, "tensor", "dp"),
            P(None, "tensor", "dp"),
            P(None, "tensor"),
            P(None, "tensor"),
            P(None, "tensor"),
            P(),
            P(),
            P(),
        ),
        out_specs=(
            P(("dp", "tensor"), None),
            P(("dp", "tensor"), None),
            P(),
            P("dp", None, "tensor"),
            P("dp", None, "tensor"),
            P("dp", None, "tensor"),
            P("tensor", "dp"),
            P("tensor", "dp"),
            P("tensor", "dp"),
            P("dp", None, "tensor"),
            P("dp", None, "tensor"),
            P("dp", None, "tensor"),
            P(None, "tensor", "dp"),
            P(None, "tensor", "dp"),
            P(None, "tensor", "dp"),
            P(None, "tensor"),
            P(None, "tensor"),
            P(None, "tensor"),
            P(),
            P(),
            P(),
        ),
        check_vma=False,
    )
```

```python
from functools import partial

import jax
import jax.numpy as jnp
import numpy as np
from jax import lax
from jax.experimental import pallas as pl
from jax.experimental.pallas import tpu as pltpu
from jax.sharding import PartitionSpec as P

HD = 64
VISIBLE = 49


norm_eps = 1e-06
beta_one = 0.9
beta_two = 0.95
adam_eps = 1e-08
clip_value = 1.0
matrix_rate = 0.02
proj_rate = 0.08
vector_rate = 0.2
matrix_decay = 0.05


def layer_norm(values, row_gain, row_shift):
    row_mean = jnp.mean(values, axis=-1, keepdims=True)
    centred = values - row_mean
    variance = jnp.mean(centred * centred, axis=-1, keepdims=True)
    return centred * lax.rsqrt(variance + norm_eps) * row_gain + row_shift


def adam_update(
    weight, gradient, first_moment, second, factor, bias_first, bias_second, learn_rate, decay_rate
):
    clipped = gradient * factor
    first_new = beta_one * first_moment + (1.0 - beta_one) * clipped
    second_new = beta_two * second + (1.0 - beta_two) * clipped * clipped
    direction = first_new / bias_first / (jnp.sqrt(second_new / bias_second) + adam_eps)
    return (weight - learn_rate * (direction + decay_rate * weight), first_new, second_new)


def transpose_dot(left_side, right_side):
    return lax.dot_general(
        left_side, right_side, (((0,), (0,)), ((), ())), preferred_element_type=jnp.float32
    )


def dot_back(left_side, right_side):
    return lax.dot_general(
        left_side, right_side, (((1,), (1,)), ((), ())), preferred_element_type=jnp.float32
    )


def square_sum(arrays):
    total = jnp.sum(arrays[0] * arrays[0])
    for member in arrays[1:]:
        total = total + jnp.sum(member * member)
    return total


def standard_normal(values):
    cumulative = 0.5 + 0.5 * lax.erf(values * (0.5**0.5))
    density = jnp.exp(-0.5 * values * values) * (0.5 / jnp.pi) ** 0.5
    return cumulative, density


every_axis = ("dp", "tensor")
low_type = jnp.bfloat16
wide_type = jnp.float32
WINDOW_IMAGES = 2
QUERY_ROWS = 112
KEY_ROWS = 128
PAIR = 2 * HD
GROUP_IMAGES = 16
GROUP_ROWS = GROUP_IMAGES * VISIBLE
WINDOWS = GROUP_IMAGES // WINDOW_IMAGES
WINDOW_UNROLL = 8
HIDDEN = -1e30


def wide(values):
    return values.astype(wide_type)


class Exchange:
    def __init__(self, dp_size, tensor_size):
        self.total = dp_size * tensor_size
        self.outer = self.total // 8
        flat_dp = lax.axis_index("dp")
        self.across = lax.axis_index("tensor")
        self.core = flat_dp & 1
        self.up = (flat_dp >> 1) & 1
        self.deep = flat_dp >> 2

    def swap(self, value, mask):
        return lax.ppermute(value, every_axis, [(i, i ^ mask) for i in range(self.total)])

    def swap_by_core(self, value, even_mask, odd_mask):
        masks = (even_mask, odd_mask)
        return lax.ppermute(
            value, every_axis, [(i, i ^ masks[(i >> 1) & 1]) for i in range(self.total)]
        )

    def digits(self):
        size = 1
        while size < self.outer:
            radix = 4 if self.outer // size >= 4 else 2
            yield size, radix
            size *= radix

    def spot(self, core, flip_second, flip_first):
        first = jnp.where(core == 0, self.up, self.across) ^ flip_first
        second = jnp.where(core == 0, self.across, self.up) ^ flip_second
        return jnp.where(core == 0, second, first), jnp.where(core == 0, first, second)


def tie(value, *others):
    return lax.optimization_barrier((value,) + tuple(jax.tree.leaves(others)))[0]


def tie_all(values, *others):
    leaves = tuple(jax.tree.leaves(others))
    return list(lax.optimization_barrier(tuple(values) + leaves)[: len(values)])


def deposit(pieces, slots):
    count = len(pieces)
    shape = (count,) + pieces[0].shape

    def kernel(spots, *refs):
        out, done = refs[count], refs[count + 1]
        copies = [
            pltpu.make_async_copy(refs[k], out.at[spots[k]], done.at[k]) for k in range(count)
        ]
        for copy in copies:
            copy.start()
        for copy in copies:
            copy.wait()

    return pl.pallas_call(
        kernel,
        out_shape=jax.ShapeDtypeStruct(shape, pieces[0].dtype),
        grid_spec=pltpu.PrefetchScalarGridSpec(
            num_scalar_prefetch=1,
            grid=(1,),
            in_specs=[pl.BlockSpec(memory_space=pl.ANY)] * count,
            out_specs=pl.BlockSpec(
                shape, lambda i, spots: (0,) * len(shape), pipeline_mode=pl.Buffered(1)
            ),
            scratch_shapes=[pltpu.SemaphoreType.DMA((count,))],
        ),
        name="deposit",
    )(jnp.stack(slots).astype(jnp.int32), *pieces)


def deposit_whole(pieces, slots, widths):
    count = len(pieces)
    outer, rows, full_width = pieces[0].shape
    starts = [sum(widths[:w]) for w in range(len(widths))]

    def kernel(spots, *refs):
        out = refs[count : count + len(widths)]
        held, came, done = refs[count + len(widths) :]
        loads = [pltpu.make_async_copy(refs[k], held.at[k], came.at[k]) for k in range(count)]
        for load in loads:
            load.start()
        stores = []
        for k in range(count):
            loads[k].wait()
            for w, width in enumerate(widths):
                cols = pl.ds(pl.multiple_of(spots[3 * k] * width, 128), width)
                source = held.at[k, :, :, pl.ds(starts[w], width)]
                target = out[w].at[:, spots[3 * k + 1], spots[3 * k + 2], :, cols]
                stores.append(pltpu.make_async_copy(source, target, done.at[k, w]))
                stores[-1].start()
        for store in stores:
            store.wait()

    shapes = [(outer, 2, 2, rows, 2 * width) for width in widths]
    flat = jnp.stack([jnp.asarray(v, jnp.int32) for slot in slots for v in slot])
    whole = pl.pallas_call(
        kernel,
        out_shape=[jax.ShapeDtypeStruct(shape, low_type) for shape in shapes],
        grid_spec=pltpu.PrefetchScalarGridSpec(
            num_scalar_prefetch=1,
            grid=(1,),
            in_specs=[pl.BlockSpec(memory_space=pl.ANY)] * count,
            out_specs=[pl.BlockSpec(memory_space=pl.ANY)] * len(widths),
            scratch_shapes=[
                pltpu.VMEM((count, outer, rows, full_width), low_type),
                pltpu.SemaphoreType.DMA((count,)),
                pltpu.SemaphoreType.DMA((count, len(widths))),
            ],
        ),
        name="deposit_whole",
    )(flat, *pieces)
    return [part.reshape(outer * 4 * rows, part.shape[-1]) for part in whole]


class Gather:
    def __init__(self, ring, name, block, widths):
        self.ring, self.name = ring, name
        self.cur, self.widths = block[None], widths

    def send_deep(self):
        with jax.named_scope(self.name + "_deep"):
            ring = self.ring
            steps = list(ring.digits())
            for size, radix in steps:
                self.spot = (ring.deep // size) % radix
                self.arrived = [ring.swap(self.cur, (k * size) << 3) for k in range(1, radix)]
                if (size, radix) != steps[-1]:
                    self.collect()

    def collect(self):
        with jax.named_scope(self.name + "_collect"):
            radix = 1 + len(self.arrived)
            stacked = deposit([self.cur] + self.arrived, [self.spot ^ k for k in range(radix)])
            self.cur = stacked.reshape((radix * self.cur.shape[0],) + self.cur.shape[1:])

    def send_beside(self):
        with jax.named_scope(self.name + "_beside"):
            self.collect()
            self.beside = self.ring.swap_by_core(self.cur, 4, 1)

    def send_far(self):
        ring, mine = self.ring, [self.cur, self.beside]
        with jax.named_scope(self.name + "_far"):
            self.far = [ring.swap_by_core(piece, 1, 4) for piece in mine]
        with jax.named_scope(self.name + "_core"):
            self.early = [ring.swap(piece, 2) for piece in mine]

    def send_core(self):
        self.mine = [self.cur, self.beside] + self.far
        with jax.named_scope(self.name + "_core"):
            self.theirs = self.early + [self.ring.swap(piece, 2) for piece in self.far]

    def whole(self):
        with jax.named_scope(self.name + "_whole"):
            ring = self.ring
            slots = []
            for core in (ring.core, 1 - ring.core):
                for flip_second in range(2):
                    for flip_first in range(2):
                        slots.append(ring.spot(core, flip_second, flip_first) + (core,))
            return deposit_whole(self.mine + self.theirs, slots, self.widths)


class Scatter:
    def __init__(self, ring, name, parts):
        self.ring, self.name = ring, name
        self.rows = parts[0].shape[0] // (ring.outer * 4)
        shape = (ring.outer, 2, 2, self.rows)
        self.views = [part.reshape(shape + part.shape[1:]) for part in parts]

    def cut(self, t, core, up=None):
        cuts = []
        for view in self.views:
            ups, width = 2 if up is None else 1, view.shape[4] // 2
            part = lax.dynamic_slice(
                view[..., t * width : (t + 1) * width],
                (0, 0 if up is None else up, core, 0, 0),
                (view.shape[0], ups, 1, view.shape[3], width),
            )
            cuts.append(part.reshape(view.shape[0], ups, view.shape[3], width))
        return cuts[0] if len(cuts) == 1 else jnp.concatenate(cuts, axis=-1)

    def send_core(self):
        with jax.named_scope(self.name + "_core"):
            self.sent = [self.cut(t, 1 - self.ring.core) for t in range(2)]
            self.arrived = [self.ring.swap(part, 2) for part in self.sent]

    def partial(self, flip_second, flip_first):
        across, up = self.ring.spot(self.ring.core, flip_second, flip_first)
        terms = [
            wide(self.cut(t, self.ring.core, up)[:, 0])
            + wide(lax.dynamic_index_in_dim(self.arrived[t], up, 1, keepdims=False))
            for t in range(2)
        ]
        return jnp.where(across == 0, terms[0], terms[1])

    def send_far(self):
        swap = self.ring.swap_by_core
        with jax.named_scope(self.name + "_far"):
            self.sent = [self.partial(1, k).astype(low_type) for k in (1, 0)]
            self.far = [swap(part, 1, 4) for part in self.sent]

    def send_near(self):
        with jax.named_scope(self.name + "_near"):
            self.sent = (self.partial(0, 1) + wide(self.far[0])).astype(low_type)
            self.near = self.ring.swap_by_core(self.sent, 4, 1)

    def send_deep(self):
        ring = self.ring
        with jax.named_scope(self.name + "_deep"):
            self.cur = self.partial(0, 0) + wide(self.far[1]) + wide(self.near)
            steps = list(reversed(list(ring.digits())))
            for size, radix in steps:
                spot = (ring.deep // size) % radix
                cur = self.cur.reshape((radix, size) + self.cur.shape[-2:])
                cut = partial(lax.dynamic_index_in_dim, axis=0, keepdims=False)
                self.sent = [cut(cur, spot ^ k).astype(low_type) for k in range(1, radix)]
                self.deep = [
                    ring.swap(part, (k * size) << 3) for k, part in enumerate(self.sent, 1)
                ]
                self.cur = cut(cur, spot)
                if (size, radix) != steps[-1]:
                    self.collect()

    def collect(self):
        for part in self.deep:
            self.cur = self.cur + wide(part)

    def finish(self):
        self.collect()
        return self.cur.reshape(self.cur.shape[1:])


def sum_everywhere(ring, value):
    bit = 1
    while bit < ring.total:
        radix = 4 if ring.total // bit >= 4 else 2
        terms = [value] + [ring.swap(value, k * bit) for k in range(1, radix)]
        while len(terms) > 1:
            terms = [terms[i] + terms[i + 1] for i in range(0, len(terms), 2)]
        value = terms[0]
        bit *= radix
    return value


def window_rows(index):
    query_start = (index * (WINDOW_IMAGES * VISIBLE)) // 16 * 16
    key_start = jnp.minimum(query_start, GROUP_ROWS - KEY_ROWS)
    return (
        pl.ds(pl.multiple_of(query_start, 16), QUERY_ROWS),
        pl.ds(pl.multiple_of(key_start, 16), KEY_ROWS),
    )


def window_masks():
    base = np.arange(WINDOWS)[:, None, None] * (WINDOW_IMAGES * VISIBLE)
    query_start = base // 16 * 16
    key_start = np.minimum(query_start, GROUP_ROWS - KEY_ROWS)
    query_at = query_start - base + np.arange(QUERY_ROWS)[None, :, None]
    key_at = key_start - base + np.arange(KEY_ROWS)[None, None, :]
    used = (query_at >= 0) & (query_at < WINDOW_IMAGES * VISIBLE)
    low_key = np.where(query_at < VISIBLE, 0, VISIBLE)
    allowed = used & (key_at >= low_key) & (key_at < low_key + VISIBLE)
    return np.where(allowed, 0.0, HIDDEN).astype(np.float32)


def split_pair(values):
    lane = lax.broadcasted_iota(jnp.int32, values.shape, 1)
    zero = jnp.zeros_like(values)
    return jnp.concatenate(
        [jnp.where(lane < HD, values, zero), jnp.where(lane >= HD, values, zero)], axis=0
    )


def join_pair(stacked):
    lane = lax.broadcasted_iota(jnp.int32, (KEY_ROWS, PAIR), 1)
    return jnp.where(lane < HD, stacked[:KEY_ROWS], stacked[KEY_ROWS:])


def over_windows(window, store):
    def several(step, carry):
        places = [step * WINDOW_UNROLL + offset for offset in range(WINDOW_UNROLL)]
        results = [window(place) for place in places]
        for place, result in zip(places, results):
            store(place, *result)
        return carry

    lax.fori_loop(0, WINDOWS // WINDOW_UNROLL, several, 0)


def head_blocks(shape, head_axis, value):
    own_axis = 1 - head_axis
    lanes = lax.broadcasted_iota(jnp.int32, shape, head_axis) < HD
    stack = lax.broadcasted_iota(jnp.int32, shape, own_axis) < KEY_ROWS
    return jnp.where(lanes == stack, value, 0.0).astype(low_type)


def attention_forward_kernel(queries, keys, values, hide, *refs):
    mixed, soft, scale = refs[-3:]
    mixed[...] = jnp.zeros_like(mixed)
    ones = head_blocks((2 * KEY_ROWS, PAIR), 1, 1.0)

    def window(index):
        query_rows, key_rows = window_rows(index)
        scaled = queries[query_rows, :] * jnp.asarray(HD**-0.5, low_type)
        scores = dot_back(scaled, split_pair(keys[key_rows, :]))
        weights = []
        for head in range(2):
            part = scores[:, head * KEY_ROWS : (head + 1) * KEY_ROWS] + hide[index]
            highest = jnp.maximum(jnp.max(part, axis=-1, keepdims=True), HIDDEN / 4)
            weights.append(jnp.exp(part - highest).astype(low_type))
        weights = jnp.concatenate(weights, axis=1)
        right = jnp.concatenate([split_pair(values[key_rows, :]), ones], axis=1)
        result = jnp.dot(weights, right, preferred_element_type=wide_type)
        total = result[:, PAIR:]
        inverse = jnp.where(total > 0.0, 1.0 / total, 0.0)
        return weights, inverse, (result[:, :PAIR] * inverse).astype(low_type)

    def store(index, weights, inverse, result):
        soft[index, 0] = weights
        scale[index, 0] = inverse
        mixed[window_rows(index)[0], :] += result

    over_windows(window, store)


def attention_backward_kernel(
    queries, keys, values, soft, scale, mixed, grad_mixed, *refs, width
):
    grad_qkv, sums = refs[-2:]
    pairs = width // PAIR
    first_col = pl.program_id(0) // pairs * (3 * width) + pl.program_id(0) % pairs * PAIR
    query_cols, key_cols, value_cols = [
        pl.ds(pl.multiple_of(first_col + part * width, PAIR), PAIR) for part in range(3)
    ]
    minus_ones = head_blocks((2 * KEY_ROWS, PAIR), 1, -1.0)
    for cols in (query_cols, key_cols, value_cols):
        grad_qkv[:, cols] = jnp.zeros((GROUP_ROWS, PAIR), low_type)
        sums[:, cols] = jnp.zeros((8, PAIR), wide_type)

    def window(index):
        query_rows, key_rows = window_rows(index)
        split_keys = split_pair(keys[key_rows, :])
        weights = soft[index, 0]
        grads = wide(grad_mixed[query_rows, :]) * scale[index, 0]
        shares = (grads * wide(mixed[query_rows, :])).astype(low_type)
        grads = grads.astype(low_type)
        left = jnp.concatenate([grads, shares], axis=1)
        right = jnp.concatenate([split_pair(values[key_rows, :]), minus_ones], axis=1)
        grad_scores = (wide(weights) * dot_back(left, right)).astype(low_type)
        grad_queries = (
            jnp.dot(grad_scores, split_keys, preferred_element_type=wide_type) * HD**-0.5
        )
        grad_keys = join_pair(transpose_dot(grad_scores, queries[query_rows, :])) * HD**-0.5
        grad_values = join_pair(transpose_dot(weights, grads))
        return (
            grad_queries.astype(low_type),
            grad_keys.astype(low_type),
            grad_values.astype(low_type),
            jnp.sum(grad_queries.reshape(-1, 8, PAIR), axis=0),
            jnp.sum(grad_values.reshape(-1, 8, PAIR), axis=0),
        )

    def store(index, grad_queries, grad_keys, grad_values, query_sums, value_sums):
        query_rows, key_rows = window_rows(index)
        grad_qkv[query_rows, query_cols] += grad_queries
        grad_qkv[key_rows, key_cols] += grad_keys
        grad_qkv[key_rows, value_cols] += grad_values
        sums[:, query_cols] += query_sums
        sums[:, value_cols] += value_sums

    over_windows(window, store)


def pair_blocks(pairs, of_group, of_pair):
    return [
        pl.BlockSpec(
            (GROUP_ROWS, PAIR),
            lambda p, k=k: (of_group, of_pair(p) // pairs * 3 * pairs + k * pairs + of_pair(p) % pairs),
        )
        for k in range(3)
    ]


def attention_forward(qkv, width, group, half, before=()):
    rows, all_width = qkv.shape[0], qkv.shape[1] // 3
    pairs, all_pairs = width // PAIR, all_width // PAIR
    hide = window_masks()
    of_pair = lambda p: half * pairs + p
    window_block = lambda p: (group, of_pair(p), 0, 0)
    return pl.pallas_call(
        attention_forward_kernel,
        grid=(pairs,),
        in_specs=pair_blocks(pairs, group, of_pair)
        + [pl.BlockSpec(hide.shape, lambda p: (0, 0, 0), pipeline_mode=pl.Buffered(1))]
        + [pl.BlockSpec(memory_space=pl.ANY)] * len(before),
        out_specs=[
            pl.BlockSpec((GROUP_ROWS, PAIR), lambda p: (group, of_pair(p))),
            pl.BlockSpec((WINDOWS, 1, QUERY_ROWS, 2 * KEY_ROWS), window_block),
            pl.BlockSpec((WINDOWS, 1, QUERY_ROWS, PAIR), window_block),
        ],
        out_shape=[
            jax.ShapeDtypeStruct((rows, all_width), low_type),
            jax.ShapeDtypeStruct(
                (rows // GROUP_ROWS * WINDOWS, all_pairs, QUERY_ROWS, 2 * KEY_ROWS), low_type
            ),
            jax.ShapeDtypeStruct(
                (rows // GROUP_ROWS * WINDOWS, all_pairs, QUERY_ROWS, PAIR), wide_type
            ),
        ],
        input_output_aliases={4 + k: k for k in range(len(before))},
        name="attention_forward",
    )(qkv, qkv, qkv, hide, *before)


def attention_backward(qkv, mixed, soft, scale, grad_mixed, width, group, before=()):
    rows, all_width = qkv.shape[0], qkv.shape[1] // 3
    pairs, all_pairs = width // PAIR, all_width // PAIR
    window_block = lambda p: (group, p, 0, 0)
    row_block = pl.BlockSpec((GROUP_ROWS, PAIR), lambda p: (group, p))
    return pl.pallas_call(
        partial(attention_backward_kernel, width=width),
        grid=(all_pairs,),
        in_specs=pair_blocks(pairs, group, lambda p: p)
        + [
            pl.BlockSpec((WINDOWS, 1, QUERY_ROWS, 2 * KEY_ROWS), window_block),
            pl.BlockSpec((WINDOWS, 1, QUERY_ROWS, PAIR), window_block),
            row_block,
            row_block,
        ]
        + [pl.BlockSpec(memory_space=pl.ANY)] * len(before),
        out_specs=[
            pl.BlockSpec((GROUP_ROWS, 3 * all_width), lambda p: (group, 0)),
            pl.BlockSpec((8, 3 * all_width), lambda p: (0, 0)),
        ],
        out_shape=[
            jax.ShapeDtypeStruct((rows, 3 * all_width), low_type),
            jax.ShapeDtypeStruct((8, 3 * all_width), wide_type),
        ],
        input_output_aliases={7: 0} if before else {},
        name="attention_backward",
    )(qkv, qkv, qkv, soft, scale, mixed, grad_mixed, *before)


def body(
    sizes,
    patches,
    visible,
    pos_table,
    cotangent,
    step_count,
    w_qkv,
    m_qkv,
    v_qkv,
    w_proj,
    m_proj,
    v_proj,
    w_fc1,
    m_fc1,
    v_fc1,
    w_fc2,
    m_fc2,
    v_fc2,
    split_bias,
    m_split,
    v_split,
    norm_bias,
    m_norm,
    v_norm,
):
    model_width = patches.shape[1]
    full_rows = patches.shape[0]
    shard_rows = w_qkv.shape[0]
    shard_width = w_qkv.shape[2]
    ring = Exchange(*sizes)

    def rows_of(proj_like):
        return jnp.swapaxes(proj_like, -1, -2)

    def low(block):
        return block.astype(low_type)

    mid_block = jnp.concatenate(
        [rows_of(w_proj), w_fc1.reshape(shard_rows, 4 * shard_width)], axis=1
    )
    fc2_block = jnp.transpose(w_fc2, (2, 0, 1)).reshape(shard_rows, 4 * shard_width)
    qkv_block = low(w_qkv.reshape(shard_rows, 3 * shard_width))
    qkv_all = Gather(ring, "qkv", qkv_block, [3 * shard_width])
    qkv_all.send_deep()
    qkv_all.send_beside()
    mid_all = Gather(
        ring, "mid", tie(low(mid_block), qkv_all.cur), [shard_width, 4 * shard_width]
    )
    mid_all.send_deep()
    qkv_all.send_far()
    qkv_all.send_core()
    fc2_all = Gather(ring, "fc2", tie(low(fc2_block), qkv_all.far), [4 * shard_width])
    fc2_all.send_deep()
    (qkv_low,) = qkv_all.whole()
    mid_all.arrived = tie_all(mid_all.arrived, qkv_low)
    mid_all.send_beside()
    other_bias = ring.swap(tie(split_bias, qkv_all.cur), 1)
    bias_halves = [jnp.where(ring.across == t, split_bias, other_bias) for t in range(2)]
    zero_bias = jnp.zeros((shard_width,), wide_type)
    qkv_shift = jnp.concatenate([v for b in bias_halves for v in (b[0], zero_bias, b[1])])
    fc1_shift = jnp.concatenate([b[2:].reshape(-1) for b in bias_halves])

    places = tie(visible, qkv_all.beside).reshape(-1)
    inputs = wide(patches) + jnp.take(pos_table, places, axis=0)
    normed, norm_back = jax.vjp(layer_norm, inputs, norm_bias[0], norm_bias[1])
    normed_low = low(normed)
    left = tie(normed_low, mid_all.cur)
    projected = low(jnp.dot(left, qkv_low, preferred_element_type=wide_type) + qkv_shift)
    groups = full_rows // GROUP_ROWS
    outcome = ()
    for call in range(2 * groups):
        source = projected
        if call == 2 * groups - 1:
            source = tie(projected, fc2_all.cur)
        outcome = attention_forward(source, shard_width, call // 2, call % 2, outcome)
        if call == 0:
            mid_all.beside = tie(mid_all.beside, outcome)
            mid_all.send_far()
        if call == 1:
            fc2_all.arrived = tie_all(fc2_all.arrived, outcome)
            fc2_all.send_beside()
        if call == 2 * groups - 1:
            mid_all.far = tie_all(mid_all.far, outcome)
            mid_all.send_core()
    mixed_low, soft_low, soft_scale = outcome
    mid_all.theirs = tie_all(mid_all.theirs, mixed_low)
    proj_low, fc1_low = mid_all.whole()
    attended = dot_back(mixed_low, proj_low)
    fc2_all.beside = tie(fc2_all.beside, attended)
    fc2_all.send_far()
    hidden_res = inputs + (attended + norm_bias[2])
    normed_two, norm_two_back = jax.vjp(layer_norm, hidden_res, norm_bias[3], norm_bias[4])
    normed_two_low = low(normed_two)
    grad_out = wide(cotangent)
    pre_gelu = jnp.dot(normed_two_low, fc1_low, preferred_element_type=wide_type) + fc1_shift
    cumulative, density = standard_normal(pre_gelu)
    activated = low(pre_gelu * cumulative)
    slope = low(cumulative + pre_gelu * density)
    fc2_all.far = tie_all(fc2_all.far, activated)
    fc2_all.send_core()
    grad_fc2 = low(transpose_dot(cotangent, activated))
    fc2_all.theirs = tie_all(fc2_all.theirs, grad_fc2)
    (fc2_low,) = fc2_all.whole()
    fc2_sum = Scatter(ring, "fc2_sum", [grad_fc2])
    fc2_sum.send_core()
    cotangent_later = tie(cotangent, fc2_sum.sent)
    grad_act = jnp.dot(cotangent_later, fc2_low, preferred_element_type=wide_type)
    grad_pre = low(grad_act * wide(slope))
    fc2_sum.arrived = tie_all(fc2_sum.arrived, grad_pre)
    fc2_sum.send_far()
    grad_fc1 = low(transpose_dot(normed_two_low, tie(grad_pre, fc2_sum.arrived)))
    fc1_sum = Scatter(ring, "fc1_sum", [grad_fc1])
    fc1_sum.send_core()
    fc2_sum.far = tie_all(fc2_sum.far, grad_fc1)
    fc2_sum.send_near()
    grad_normed_two = dot_back(tie(grad_pre, fc1_sum.sent, fc2_sum.far), fc1_low)
    fc2_sum.near = tie(fc2_sum.near, grad_normed_two)
    fc2_sum.send_deep()
    fc1_sum.arrived = tie_all(fc1_sum.arrived, grad_normed_two)
    fc1_sum.send_far()
    grad_hidden_norm, grad_gain_two, grad_shift_two = norm_two_back(
        tie(grad_normed_two, fc1_sum.arrived, fc2_sum.near)
    )
    grad_hidden = grad_out + grad_hidden_norm
    grad_attn_low = low(grad_hidden)
    grad_proj = low(transpose_dot(grad_attn_low, mixed_low))
    grad_mixed = low(jnp.dot(grad_attn_low, proj_low, preferred_element_type=wide_type))
    fc2_shard = fc2_sum.finish()
    gradient, column_sums = (), 0.0
    for group in range(groups):
        if group == 0:
            source = tie(grad_mixed, grad_proj)
        else:
            source = tie(grad_mixed, fc1_sum.sent)
        *gradient, sums = attention_backward(
            projected, mixed_low, soft_low, soft_scale, source, shard_width, group, gradient
        )
        column_sums = column_sums + jnp.sum(sums, axis=0)
        if group == 0:
            fc1_sum.far = tie_all(fc1_sum.far, gradient)
            fc1_sum.send_near()
        elif group == groups - 1:
            fc1_sum.near = tie(fc1_sum.near, gradient)
            fc1_sum.send_deep()
    (grad_projected,) = gradient
    grad_qkv = low(transpose_dot(normed_low, grad_projected))
    front_sum = Scatter(ring, "front_sum", [grad_qkv, grad_proj])
    front_sum.send_core()
    out_column_sums = jnp.stack(
        [
            jnp.sum(wide(values), axis=0)
            for values in tie_all([grad_attn_low, cotangent], front_sum.sent)
        ]
    )
    grad_fc1_bias = jnp.sum(wide(tie(grad_pre, front_sum.sent)), axis=0)
    front_sum.arrived = tie_all(front_sum.arrived, out_column_sums, grad_fc1_bias)
    front_sum.send_far()
    ffn_out = dot_back(tie(activated, front_sum.sent), fc2_low) + norm_bias[5]
    block_out = low(hidden_res + ffn_out)
    front_sum.far = tie_all(front_sum.far, block_out)
    front_sum.send_near()
    grad_normed = dot_back(tie(grad_projected, front_sum.sent), qkv_low)
    front_sum.near = tie(front_sum.near, grad_normed)
    front_sum.send_deep()
    grad_normed = tie(grad_normed, front_sum.sent)
    fc1_sum.deep = tie_all(fc1_sum.deep, grad_normed)
    fc1_shard = fc1_sum.finish()
    grad_input_norm, grad_gain_one, grad_shift_one = norm_back(grad_normed)
    input_grad = grad_hidden + grad_input_norm
    column_sums = column_sums.reshape(2, 3, shard_width)
    grad_split = jnp.concatenate(
        [
            column_sums[:, 0].reshape(1, -1),
            column_sums[:, 2].reshape(1, -1),
            jnp.swapaxes(grad_fc1_bias.reshape(2, 4, shard_width), 0, 1).reshape(4, -1),
        ]
    )
    grad_norm_rows = jnp.stack(
        [
            grad_gain_one,
            grad_shift_one,
            out_column_sums[0],
            grad_gain_two,
            grad_shift_two,
            out_column_sums[1],
        ]
    )
    front_sum.deep = tie_all(front_sum.deep, input_grad, grad_norm_rows)
    front_shard = front_sum.finish()
    shards = (
        front_shard[:, : 3 * shard_width].reshape(shard_rows, 3, shard_width),
        rows_of(front_shard[:, 3 * shard_width :]),
        fc1_shard.reshape(shard_rows, 4, shard_width),
        jnp.transpose(fc2_shard.reshape(shard_rows, 4, shard_width), (1, 2, 0)),
    )
    local_square = square_sum((front_shard, fc1_shard, fc2_shard))
    vectors = jnp.concatenate(
        [grad_norm_rows, grad_split, jnp.full((4, model_width), local_square)]
    )
    vectors = sum_everywhere(ring, vectors)
    norm_total, split_whole, square_total = vectors[:6], vectors[6:12], vectors[12, 0]
    vectors = vectors[:12]
    split_total = jnp.where(
        ring.across == 0, split_whole[:, :shard_width], split_whole[:, shard_width:]
    )
    grad_norm = jnp.sqrt(square_total + jnp.sum(vectors * vectors))
    factor = jnp.minimum(1.0, clip_value / (grad_norm + 1e-06))
    step_value = step_count[0].astype(jnp.float32)
    bias_first = 1.0 - jnp.power(beta_one, step_value)
    bias_second = 1.0 - jnp.power(beta_two, step_value)
    qkv_out = adam_update(
        w_qkv, shards[0], m_qkv, v_qkv, factor, bias_first, bias_second, matrix_rate, matrix_decay
    )
    proj_out = adam_update(
        w_proj, shards[1], m_proj, v_proj, factor, bias_first, bias_second, proj_rate, matrix_decay
    )
    fc1_out = adam_update(
        w_fc1, shards[2], m_fc1, v_fc1, factor, bias_first, bias_second, matrix_rate, matrix_decay
    )
    fc2_out = adam_update(
        w_fc2, shards[3], m_fc2, v_fc2, factor, bias_first, bias_second, matrix_rate, matrix_decay
    )
    split_out = adam_update(
        split_bias, split_total, m_split, v_split, factor, bias_first, bias_second, vector_rate, 0.0
    )
    norm_out = adam_update(
        norm_bias, norm_total, m_norm, v_norm, factor, bias_first, bias_second, vector_rate, 0.0
    )
    return (
        block_out,
        input_grad,
        grad_norm,
        qkv_out[0],
        qkv_out[1],
        qkv_out[2],
        proj_out[0],
        proj_out[1],
        proj_out[2],
        fc1_out[0],
        fc1_out[1],
        fc1_out[2],
        fc2_out[0],
        fc2_out[1],
        fc2_out[2],
        split_out[0],
        split_out[1],
        split_out[2],
        norm_out[0],
        norm_out[1],
        norm_out[2],
    )


def solution(mesh):
    sizes = (mesh.shape["dp"], mesh.shape["tensor"])
    return jax.shard_map(
        partial(body, sizes),
        mesh=mesh,
        in_specs=(
            P(("dp", "tensor"), None),
            P(("dp", "tensor"), None),
            P(),
            P(("dp", "tensor"), None),
            P(),
            P("dp", None, "tensor"),
            P("dp", None, "tensor"),
            P("dp", None, "tensor"),
            P("tensor", "dp"),
            P("tensor", "dp"),
            P("tensor", "dp"),
            P("dp", None, "tensor"),
            P("dp", None, "tensor"),
            P("dp", None, "tensor"),
            P(None, "tensor", "dp"),
            P(None, "tensor", "dp"),
            P(None, "tensor", "dp"),
            P(None, "tensor"),
            P(None, "tensor"),
            P(None, "tensor"),
            P(),
            P(),
            P(),
        ),
        out_specs=(
            P(("dp", "tensor"), None),
            P(("dp", "tensor"), None),
            P(),
            P("dp", None, "tensor"),
            P("dp", None, "tensor"),
            P("dp", None, "tensor"),
            P("tensor", "dp"),
            P("tensor", "dp"),
            P("tensor", "dp"),
            P("dp", None, "tensor"),
            P("dp", None, "tensor"),
            P("dp", None, "tensor"),
            P(None, "tensor", "dp"),
            P(None, "tensor", "dp"),
            P(None, "tensor", "dp"),
            P(None, "tensor"),
            P(None, "tensor"),
            P(None, "tensor"),
            P(),
            P(),
            P(),
        ),
        check_vma=False,
    )
```
